32 devices in a mesh: shard: 4 (over x, core), ctx: 2 (over y), tp: 4 (over z).
Axes of the slice: x: 2, y: 2, z: 4, core: 2. Of those that a mesh axis runs over, the one named last changes fastest.
Arguments:
- tokens: bfloat16 [4096, 1024], P(('shard', 'ctx')), may hold values from -6 to 6
- cotangent: bfloat16 [4096, 1024], P(('shard', 'ctx')), may hold values from -6 to 6
- segment_ids: int32 [4, 1024], P('shard'), may hold values from 0 to 15, never falling along the last dimension, each value on 1 to 512 neighbouring positions
- routes: int32 [4096, 2], P(('shard', 'ctx')), may hold values from 0 to 3, all different within a row
- pair_order: int32 [4096, 2], P(('shard', 'ctx')), may hold values from 0 to 1023, as said below
- rel_bucket: int32 [2047], replicated, may hold values from 0 to 31
- attn_gain: bfloat16 [1024], P(('shard', 'ctx')), may hold values from 0.5 to 1.5
- w_query: bfloat16 [1024, 1024], P(('shard', 'ctx'), 'tp'), may hold values from -0.1875 to 0.1875
- w_key: bfloat16 [1024, 1024], P(('shard', 'ctx'), 'tp'), may hold values from -0.1875 to 0.1875
- w_value: bfloat16 [1024, 1024], P(('shard', 'ctx'), 'tp'), may hold values from -0.1875 to 0.1875
- w_output: bfloat16 [1024, 1024], P(('shard', 'ctx'), 'tp'), may hold values from -0.75 to 0.75
- bias_table: bfloat16 [32, 16], P(None, 'tp'), may hold values from -4 to 4
- ffn_gain: bfloat16 [1024], P(('shard', 'ctx')), may hold values from 0.5 to 1.5
- w_router: bfloat16 [1024, 4], P(('shard', 'ctx')), may hold values from -0.1875 to 0.1875
- expert_gate: bfloat16 [4, 1024, 2816], P('shard', 'ctx', 'tp'), may hold values from -0.1875 to 0.1875
- expert_up: bfloat16 [4, 1024, 2816], P('shard', 'ctx', 'tp'), may hold values from -0.1875 to 0.1875
- expert_down: bfloat16 [4, 1024, 2816], P('shard', 'ctx', 'tp'), may hold values from -0.109375 to 0.109375
Outputs:
- layer_out: bfloat16 [4096, 1024], P(('shard', 'ctx'))
- tokens_grad: float32 [4096, 1024], P(('shard', 'ctx'))
- attn_gain_grad: float32 [1024], P(('shard', 'ctx'))
- w_query_grad: float32 [1024, 1024], P(('shard', 'ctx'), 'tp')
- w_key_grad: float32 [1024, 1024], P(('shard', 'ctx'), 'tp')
- w_value_grad: float32 [1024, 1024], P(('shard', 'ctx'), 'tp')
- w_output_grad: float32 [1024, 1024], P(('shard', 'ctx'), 'tp')
- bias_table_grad: float32 [32, 16], P(None, 'tp')
- ffn_gain_grad: float32 [1024], P(('shard', 'ctx'))
- w_router_grad: float32 [1024, 4], P(('shard', 'ctx'))
- expert_gate_grad: float32 [4, 1024, 2816], P('shard', 'ctx', 'tp')
- expert_up_grad: float32 [4, 1024, 2816], P('shard', 'ctx', 'tp')
- expert_down_grad: float32 [4, 1024, 2816], P('shard', 'ctx', 'tp')
The draws below stay inside these ranges and needn't reach their ends.
Inputs may be any that keep to these rules, and one draw needn't show every extreme that they name: `segment_ids`: along each row the numbers never fall. `routes`: the two experts of a row differ. `pair_order`: the 1024 entries of each aligned block of 512 rows are a permutation of 0 to 1023.
All inputs are finite; a program needn't handle non-finite values.
Results may differ from the reference program's by a relative error of at most 0.017.
Values may be sent and summed in bfloat16 or wider, within the bound.
No kernel may reach another device: no remote copies, remote signals or barrier semaphores. Data moves between devices by JAX's collectives and lax.ppermute only.
A program may use at most 192 MiB of HBM per device.

```python
import math
import jax
import jax.numpy as jnp
import numpy as np
from jax import lax

D = 1024
HEADS = 16
HEAD_DIM = 64
FF = 2816
BUCKETS = 32
TOP = 2
SEQ = 1024
EXPERTS = 4
SEQS = 4
TOKENS = 4096
TOK_DEV = 512
BLOCKS = 8
CAP = 288


def shuffled_block(block_key):
    return jax.random.permutation(block_key, TOP * TOK_DEV)


def draw_pair_order(key, part):
    block_keys = jax.random.split(jax.random.fold_in(key, 7), BLOCKS)
    ranking = jax.vmap(shuffled_block)(block_keys)
    return ranking.reshape(BLOCKS * TOK_DEV, TOP).astype(jnp.int32)


def touch_ends(values, rng, low, high):
    spot = [jax.random.randint(jax.random.fold_in(rng, axis), (), 0, length) for axis, length in enumerate(values.shape)]
    main_axis = values.shape.index(max(values.shape))
    next_to = spot[:main_axis] + [(spot[main_axis] + 1) % values.shape[main_axis]] + spot[main_axis + 1:]
    return values.at[tuple(spot)].set(low).at[tuple(next_to)].set(high)


def level_of(rng, extent, pieces, smallest, top_value):
    def one(dim, shards_of):
        steps = jax.random.uniform(jax.random.fold_in(jax.random.fold_in(rng, 6), dim), (shards_of,), jnp.float32, smallest / len(pieces), top_value / len(pieces))
        return jnp.repeat(jnp.exp(steps), extent[dim] // shards_of).reshape((-1,) + (1,) * (len(extent) - dim - 1))

    gain = one(*pieces[0])
    for cut in pieces[1:]:
        gain = gain * one(*cut)
    return gain


def picks_of(key, rows, count, top, lift):
    order = jax.random.permutation(jax.random.fold_in(key, 1), count)
    boost = order
    for power in range(3):
        boost = boost * boost // count
    boost = boost * lift // count
    tickets = jax.random.randint(jax.random.fold_in(key, 2), (rows, count), 0, 4096) + boost
    sure = jax.random.permutation(jax.random.fold_in(key, 3), rows)[jnp.arange(count) % rows]
    tickets = jnp.where(jnp.arange(rows)[:, None] == sure[None, :], 1 << 14, tickets)
    merit = tickets * count + jnp.arange(count)
    return lax.top_k(merit.astype(jnp.int32), top)[1].astype(jnp.int32)


def split_up(count, total, bound, slope):
    loads = [(1 << 20) // math.isqrt(grade ** slope) + 1 for grade in range(2, count + 1)]
    spare, holding = total - bound - (count - 1), [1] * (count - 1)
    while spare > 0:
        candidates = [i for i in range(count - 1) if holding[i] < bound]
        pool, remaining = sum([loads[i] for i in candidates]), spare
        for i in candidates:
            addition = min(bound - holding[i], max(1, remaining * loads[i] // pool), spare)
            holding[i] = holding[i] + addition
            spare = spare - addition
    return np.array([bound] + holding)


def uneven(rng, number_of, total, reach, lean):
    if number_of == 2:
        one = jax.random.randint(rng, (), max(1, total - reach), min(reach, total - 1) + 1)
        return jnp.stack([one, total - one])
    tallies = jnp.asarray(split_up(number_of, total, reach, lean), jnp.int32)
    pairs = (number_of - 1) // 2
    donor, receiver = tallies[1:1 + 2 * pairs:2], tallies[2:2 + 2 * pairs:2]
    room = jnp.minimum(donor - 1, reach - receiver)
    shifted = jax.random.randint(jax.random.fold_in(rng, 1), (pairs,), 0, 1 << 20) % (room + 1)
    tallies = tallies.at[1:1 + 2 * pairs:2].set(donor - shifted).at[2:2 + 2 * pairs:2].set(receiver + shifted)
    return tallies[jax.random.permutation(jax.random.fold_in(rng, 2), number_of)]


def gaussian(own_key, dims, deviation, most, cuts=(), held_as=jnp.bfloat16):
    loudness = level_of(own_key, dims, cuts, -0.22, 0.18) if cuts else 1.0
    array = jax.random.normal(own_key, dims, jnp.float32) * deviation * loudness
    return jnp.minimum(jnp.maximum(array, -most), most).astype(held_as)


def setup_inputs(seed: int = 0) -> dict:
    seeds = jax.random.split(jax.random.key(seed), 18)
    return {
        "tokens": gaussian(seeds[0], (TOKENS, D), 1.0, 6.0, ((0, 8),)),
        "cotangent": gaussian(seeds[1], (TOKENS, D), 1.0, 6.0, ((0, 8),)),
        "segment_ids": jax.vmap(lambda own: jnp.searchsorted(jnp.cumsum(uneven(own, 16, SEQ, SEQ // 2, 2)), jnp.arange(SEQ), side="right"))(jax.random.split(seeds[2], SEQS)).reshape((SEQS, SEQ)).astype(jnp.int32),
        "routes": picks_of(seeds[3], TOKENS, EXPERTS, TOP, 4096),
        "pair_order": draw_pair_order(jax.random.fold_in(seeds[17], 71), 0),
        "rel_bucket": touch_ends(jax.random.randint(seeds[5], (2 * SEQ - 1,), 0, BUCKETS), jax.random.fold_in(seeds[5], 1), 0, BUCKETS - 1).astype(jnp.int32),
        "attn_gain": jnp.clip(1.0 + 0.1 * jax.random.normal(seeds[6], (D,), jnp.float32), 0.5, 1.5).astype(jnp.bfloat16),
        "w_query": gaussian(seeds[7], (D, HEADS * HEAD_DIM), D ** -0.5, 0.1875, ((0, 8), (1, 4))),
        "w_key": gaussian(seeds[8], (D, HEADS * HEAD_DIM), D ** -0.5, 0.1875, ((0, 8), (1, 4))),
        "w_value": gaussian(seeds[9], (D, HEADS * HEAD_DIM), D ** -0.5, 0.1875, ((0, 8), (1, 4))),
        "w_output": gaussian(seeds[10], (D, HEADS * HEAD_DIM), (HEADS * HEAD_DIM // 16) ** -0.5, 0.75, ((0, 8), (1, 4))),
        "bias_table": gaussian(seeds[11], (BUCKETS, HEADS), 1.0, 4.0, ((1, 4),)),
        "ffn_gain": jnp.clip(1.0 + 0.1 * jax.random.normal(seeds[12], (D,), jnp.float32), 0.5, 1.5).astype(jnp.bfloat16),
        "w_router": gaussian(seeds[13], (D, EXPERTS), D ** -0.5, 0.1875, ((0, 8),)),
        "expert_gate": gaussian(seeds[14], (EXPERTS, D, FF), D ** -0.5, 0.1875, ((0, 4), (1, 2), (2, 4))),
        "expert_up": gaussian(seeds[15], (EXPERTS, D, FF), D ** -0.5, 0.1875, ((0, 4), (1, 2), (2, 4))),
        "expert_down": gaussian(seeds[16], (EXPERTS, D, FF), FF ** -0.5, 0.109375, ((0, 4), (1, 2), (2, 4))),
    }


EPSILON = 1e-06
NEGATIVE = -1e+30
HIGHEST_PRECISION = lax.Precision.HIGHEST

@jax.custom_vjp
def low(v):
    return lax.optimization_barrier(v.astype(jnp.bfloat16)).astype(jnp.float32)

@jax.custom_vjp
def low_back(v):
    return v

def low_keep(v):
    return (low(v), None)

def low_pass(kept, grad):
    return (grad,)

def back_keep(v):
    return (v, None)

def back_low(kept, grad):
    return (low(grad),)
low.defvjp(low_keep, low_pass)
low_back.defvjp(back_keep, back_low)

def rms_norm(features_in, gain_row):
    inv_root = lax.rsqrt(lax.optimization_barrier(jnp.mean(features_in * features_in, axis=-1, keepdims=True)) + EPSILON)
    return features_in * inv_root * gain_row

def place_pairs(routes, pair_order, experts, capacity):
    pair_count = routes.shape[0] * routes.shape[1]
    flat_route = routes.reshape(pair_count)
    flat_order = pair_order.reshape(pair_count)
    onehot = (flat_route[:, None] == jnp.arange(experts, dtype=jnp.int32)[None, :]).astype(jnp.int32)
    arranged = jnp.zeros((pair_count, experts), jnp.int32).at[flat_order].set(onehot)
    earlier = jnp.cumsum(arranged, axis=0, dtype=jnp.int32) - arranged
    position = lax.optimization_barrier(jnp.sum(earlier[flat_order] * onehot, axis=1, dtype=jnp.int32))
    accepted = position < capacity
    slot_index = jnp.where(accepted, flat_route * capacity + position, experts * capacity)
    return (slot_index.reshape(routes.shape).astype(jnp.int32), accepted.reshape(routes.shape))

def place_block(block_routes, block_order):
    return place_pairs(block_routes, block_order, EXPERTS, CAP)

def block_tokens(slot_index):
    slot_count = EXPERTS * CAP
    token_of_pair = jnp.repeat(jnp.arange(TOK_DEV, dtype=jnp.int32), TOP)
    filled = jnp.full((slot_count + 1,), TOK_DEV, jnp.int32).at[slot_index.reshape(-1)].set(token_of_pair)
    return filled[:slot_count]

def sequence_attention(queries, key_rows, values, segments, relative):
    length = queries.shape[0]
    score_scale = 1.0 / math.sqrt(queries.shape[2])
    positions = jnp.arange(length, dtype=jnp.int32)
    offsets = positions[None, :] - positions[:, None] + (length - 1)
    bias_terms = jnp.transpose(relative[offsets], (2, 0, 1))
    scores = jnp.einsum('qhd,khd->hqk', queries, key_rows, precision=HIGHEST_PRECISION) * score_scale + bias_terms
    allowed = segments[:, None] == segments[None, :]
    scores = low_back(jnp.where(allowed[None], scores, NEGATIVE))
    probabilities = low(jax.nn.softmax(scores, axis=-1))
    context = jnp.einsum('hqk,khd->qhd', probabilities, values, precision=HIGHEST_PRECISION)
    return low_back(low(context))

def expert_block(expert_rows, gate_w, up_w, down_w):
    gate_pre = low_back(jnp.dot(expert_rows, gate_w, precision=HIGHEST_PRECISION))
    up_pre = low_back(jnp.dot(expert_rows, up_w, precision=HIGHEST_PRECISION))
    activated = low_back(low(jax.nn.gelu(gate_pre, approximate=True) * up_pre))
    return low_back(jnp.dot(activated, down_w.T, precision=HIGHEST_PRECISION))

def reference(tokens, cotangent, segment_ids, routes, pair_order, rel_bucket, attn_gain, w_query, w_key, w_value, w_output, bias_table, ffn_gain, w_router, expert_gate, expert_up, expert_down):
    slot_index, accepted = jax.vmap(place_block)(routes.reshape(BLOCKS, TOK_DEV, TOP), pair_order.reshape(BLOCKS, TOK_DEV, TOP))
    local_tokens = jax.vmap(block_tokens)(slot_index)
    block_base = jnp.arange(BLOCKS, dtype=jnp.int32)[:, None] * TOK_DEV
    global_tokens = jnp.where(local_tokens < TOK_DEV, local_tokens + block_base, TOKENS)
    expert_token = jnp.transpose(global_tokens.reshape(BLOCKS, EXPERTS, CAP), (1, 0, 2)).reshape(EXPERTS, BLOCKS * CAP)
    slot_expert = slot_index // CAP
    slot_place = slot_index % CAP
    block_number = jnp.arange(BLOCKS, dtype=jnp.int32)[:, None, None]
    pair_index = jnp.where(accepted, slot_expert * (BLOCKS * CAP) + block_number * CAP + slot_place, EXPERTS * BLOCKS * CAP)
    pair_index = pair_index.reshape(TOKENS, TOP).astype(jnp.int32)

    def forward(rows_in, gain_one, query_w, key_w, value_w, output_w, table, gain_two, router_w, gate_w, up_w, down_w):
        normed = low(rms_norm(rows_in, gain_one))
        queries = low_back(low(jnp.dot(normed, query_w, precision=HIGHEST_PRECISION)))
        key_rows = low_back(low(jnp.dot(normed, key_w, precision=HIGHEST_PRECISION)))
        values = low_back(low(jnp.dot(normed, value_w, precision=HIGHEST_PRECISION)))
        relative = table[rel_bucket]

        def one_sequence(carried, inputs):
            seq_queries, seq_keys, seq_values, seq_segments = inputs
            return (carried, sequence_attention(seq_queries, seq_keys, seq_values, seq_segments, relative))
        shaped = (SEQS, SEQ, HEADS, HEAD_DIM)
        _, attended = lax.scan(jax.checkpoint(one_sequence), None, (queries.reshape(shaped), key_rows.reshape(shaped), values.reshape(shaped), segment_ids))
        attended = attended.reshape(TOKENS, HEADS * HEAD_DIM)
        branch = low_back(jnp.dot(attended, output_w.T, precision=HIGHEST_PRECISION))
        hidden = rows_in + branch
        normed_two = rms_norm(hidden, gain_two)
        moe_in = low(normed_two)
        logits = low_back(jnp.dot(moe_in, router_w, precision=HIGHEST_PRECISION))
        chosen = jnp.take_along_axis(logits, routes, axis=1)
        gate_values = jax.nn.softmax(chosen, axis=1)
        padded_in = jnp.concatenate((moe_in, jnp.zeros((1, D), jnp.float32)), axis=0)

        def one_expert(inputs):
            token_index, expert_gate_w, expert_up_w, expert_down_w = inputs
            return expert_block(padded_in[token_index], expert_gate_w, expert_up_w, expert_down_w)
        expert_out = lax.map(jax.checkpoint(one_expert), (expert_token, gate_w, up_w, down_w))
        flat_out = jnp.concatenate((expert_out.reshape(EXPERTS * BLOCKS * CAP, D), jnp.zeros((1, D), jnp.float32)), axis=0)
        pair_out = flat_out[pair_index]
        return hidden + lax.optimization_barrier(jnp.sum(gate_values[:, :, None] * pair_out, axis=1))
    float_args = (tokens.astype(jnp.float32), attn_gain.astype(jnp.float32), w_query.astype(jnp.float32), w_key.astype(jnp.float32), w_value.astype(jnp.float32), w_output.astype(jnp.float32), bias_table.astype(jnp.float32), ffn_gain.astype(jnp.float32), w_router.astype(jnp.float32), expert_gate.astype(jnp.float32), expert_up.astype(jnp.float32), expert_down.astype(jnp.float32))
    layer_out, pullback = jax.vjp(forward, float_args[0], float_args[1], float_args[2], float_args[3], float_args[4], float_args[5], float_args[6], float_args[7], float_args[8], float_args[9], float_args[10], float_args[11])
    gradients = pullback(cotangent.astype(jnp.float32))
    return (layer_out.astype(jnp.bfloat16), gradients[0], gradients[1], gradients[2], gradients[3], gradients[4], gradients[5], gradients[6], gradients[7], gradients[8], gradients[9], gradients[10], gradients[11])
```

```python
import jax
import jax.numpy as jnp
from jax import lax
from jax.experimental import pallas as pl
from jax.experimental.pallas import tpu as pltpu
from jax.sharding import PartitionSpec as P

HEAD_DIM = 64
EPSILON = 1e-06
NEGATIVE = -1e30
HIGHEST_PRECISION = lax.Precision.HIGHEST
HALVES = 2


def toeplitz(window_row, rows, width):
    spread = jnp.broadcast_to(window_row, (rows, window_row.shape[1]))
    turned = pltpu.roll(spread, width - rows + 1, 1, stride=1, stride_axis=0)
    return turned


def attend_kernel(query_ref, key_own, value_own, key_far, value_far, seg_row, seg_own, seg_far, near_ref, far_ref, out_ref, total_ref, bias, kept):
    rows = 128
    length = key_own.shape[0]
    blocks = length // rows
    width = near_ref.shape[-1]
    for head in range(2):
        lanes = slice(head * HEAD_DIM, (head + 1) * HEAD_DIM)
        query = query_ref[lanes, :]
        bias[0] = toeplitz(near_ref[0, head : head + 1, :], rows, width)
        bias[1] = toeplitz(far_ref[0, head : head + 1, :], rows, width)
        highest = None
        for part in range(2):
            keys, segs = ((key_own, seg_own), (key_far, seg_far))[part]
            for block in range(blocks):
                span = slice(block * rows, (block + 1) * rows)
                first = (blocks - 1 - block) * rows
                scores = jnp.dot(keys[span, lanes], query, preferred_element_type=jnp.float32)
                scores = scores + bias[part, :, first : first + length]
                scores = jnp.where(segs[span, :] == seg_row[...], scores, NEGATIVE)
                kept[part * blocks + block] = scores
                top = jnp.max(scores, axis=0, keepdims=True)
                highest = top if highest is None else jnp.maximum(highest, top)
        total = None
        context = None
        for part in range(2):
            vals = (value_own, value_far)[part]
            for block in range(blocks):
                span = slice(block * rows, (block + 1) * rows)
                grown = jnp.exp(kept[part * blocks + block] - highest)
                added = jnp.sum(grown, axis=0, keepdims=True)
                total = added if total is None else total + added
                more = lax.dot_general(
                    vals[span, lanes], grown.astype(jnp.bfloat16), (((0,), (0,)), ((), ())),
                    preferred_element_type=jnp.float32,
                )
                context = more if context is None else context + more
        result = (context / total).astype(jnp.bfloat16)
        chunk = out_ref.shape[2]
        for index in range(out_ref.shape[0]):
            out_ref[index, lanes, :] = result[:, index * chunk : (index + 1) * chunk]
        total_ref[0, head : head + 1, :] = highest + jnp.log(total)


def attend_back_kernel(query_ref, grad_ref, key_own, value_own, key_far, value_far, seg_row, seg_own, seg_far, near_ref, far_ref, total_ref,
                       grad_query, key_grad_own, value_grad_own, key_grad_far, value_grad_far, band_ref, bias, kept, slopes, gathered):
    rows = 128
    length = key_own.shape[0]
    blocks = length // rows
    width = near_ref.shape[-1]
    across = (((1,), (1,)), ((), ()))
    down = (((0,), (0,)), ((), ()))
    for head in range(2):
        lanes = slice(head * HEAD_DIM, (head + 1) * HEAD_DIM)
        query = query_ref[lanes, :]
        grads = jnp.concatenate([grad_ref[index, lanes, :] for index in range(grad_ref.shape[0])], axis=1)
        log_total = total_ref[0, head : head + 1, :]
        bias[0] = toeplitz(near_ref[0, head : head + 1, :], rows, width)
        bias[1] = toeplitz(far_ref[0, head : head + 1, :], rows, width)
        shared = None
        for part in range(2):
            keys, vals, segs, value_grad = (
                (key_own, value_own, seg_own, value_grad_own), (key_far, value_far, seg_far, value_grad_far),
            )[part]
            for block in range(blocks):
                span = slice(block * rows, (block + 1) * rows)
                first = (blocks - 1 - block) * rows
                scores = jnp.dot(keys[span, lanes], query, preferred_element_type=jnp.float32)
                scores = scores + bias[part, :, first : first + length]
                scores = jnp.where(segs[span, :] == seg_row[...], scores, NEGATIVE)
                probs = jnp.exp(scores - log_total)
                slope = jnp.dot(vals[span, lanes], grads, preferred_element_type=jnp.float32)
                value_grad[span, lanes] = lax.dot_general(
                    probs.astype(jnp.bfloat16), grads, across, preferred_element_type=jnp.float32
                ).astype(value_grad.dtype)
                kept[part * blocks + block] = probs
                slopes[part * blocks + block] = slope
                added = jnp.sum(probs * slope, axis=0, keepdims=True)
                shared = added if shared is None else shared + added
        query_grad = None
        for part in range(2):
            keys, key_grad = ((key_own, key_grad_own), (key_far, key_grad_far))[part]
            gathered[...] = jnp.zeros_like(gathered)
            for block in range(blocks):
                span = slice(block * rows, (block + 1) * rows)
                first = (blocks - 1 - block) * rows
                change = kept[part * blocks + block] * (slopes[part * blocks + block] - shared)
                gathered[:, first : first + length] += change
                low = change.astype(jnp.bfloat16)
                key_grad[span, lanes] = lax.dot_general(
                    low, query, across, preferred_element_type=jnp.float32
                ).astype(key_grad.dtype)
                more = lax.dot_general(keys[span, lanes], low, down, preferred_element_type=jnp.float32)
                query_grad = more if query_grad is None else query_grad + more
            flip = (
                lax.broadcasted_iota(jnp.int32, (rows, rows), 0) + lax.broadcasted_iota(jnp.int32, (rows, rows), 1) == rows - 1
            ).astype(jnp.float32)
            turned = jnp.dot(flip, gathered[...], precision=HIGHEST_PRECISION, preferred_element_type=jnp.float32)
            turned = pltpu.roll(turned, 0, 1, stride=1, stride_axis=0)
            band_ref[0, 2 * part + head : 2 * part + head + 1, :] = jnp.sum(turned, axis=0, keepdims=True)
        grad_query[lanes, :] = (query_grad * 0.125).astype(jnp.bfloat16)


def whole(array):
    zeros = (0,) * array.ndim
    return pl.BlockSpec(array.shape, lambda pair: zeros)


def attend(query_rows, own, far, seg_row, seg_own, seg_far, near, beyond, pieces):
    features, length = query_rows.shape
    pairs = features // 128
    both = pl.BlockSpec((128, length), lambda pair: (pair, 0))
    keys = pl.BlockSpec((length, 128), lambda pair: (0, pair))
    vals = pl.BlockSpec((length, 128), lambda pair: (0, pairs + pair))
    window = pl.BlockSpec((1, 2, near.shape[-1]), lambda pair: (pair, 0, 0))
    return pl.pallas_call(
        attend_kernel,
        grid=(pairs,),
        in_specs=[both, keys, vals, keys, vals, whole(seg_row), whole(seg_own), whole(seg_far), window, window],
        out_specs=[pl.BlockSpec((pieces, 128, length // pieces), lambda pair: (0, pair, 0)), pl.BlockSpec((1, 2, length), lambda pair: (pair, 0, 0))],
        out_shape=[
            jax.ShapeDtypeStruct((pieces, features, length // pieces), jnp.bfloat16),
            jax.ShapeDtypeStruct((pairs, 2, length), jnp.float32),
        ],
        scratch_shapes=[
            pltpu.VMEM((2, 128, near.shape[-1]), jnp.float32),
            pltpu.VMEM((2 * length // 128, 128, length), jnp.float32),
        ],
        name="attend",
    )(query_rows, own, own, far, far, seg_row, seg_own, seg_far, near, beyond)


def attend_back(query_rows, grad_rows, own, far, seg_row, seg_own, seg_far, near, beyond, log_totals):
    features, length = query_rows.shape
    pairs = features // 128
    both = pl.BlockSpec((128, length), lambda pair: (pair, 0))
    keys = pl.BlockSpec((length, 128), lambda pair: (0, pair))
    vals = pl.BlockSpec((length, 128), lambda pair: (0, pairs + pair))
    window = pl.BlockSpec((1, 2, near.shape[-1]), lambda pair: (pair, 0, 0))
    tall = lambda kind: jax.ShapeDtypeStruct((length, features), kind)
    return pl.pallas_call(
        attend_back_kernel,
        grid=(pairs,),
        in_specs=[both, pl.BlockSpec((grad_rows.shape[0], 128, grad_rows.shape[2]), lambda pair: (0, pair, 0)), keys, vals, keys, vals, whole(seg_row), whole(seg_own), whole(seg_far), window, window,
                  pl.BlockSpec((1, 2, length), lambda pair: (pair, 0, 0))],
        out_specs=[both, keys, keys, keys, keys, pl.BlockSpec((1, 4, near.shape[-1]), lambda pair: (pair, 0, 0))],
        out_shape=[
            jax.ShapeDtypeStruct((features, length), jnp.bfloat16),
            tall(jnp.float32), tall(jnp.float32), tall(jnp.bfloat16), tall(jnp.bfloat16),
            jax.ShapeDtypeStruct((pairs, 4, near.shape[-1]), jnp.float32),
        ],
        scratch_shapes=[
            pltpu.VMEM((2, 128, near.shape[-1]), jnp.float32),
            pltpu.VMEM((2 * length // 128, 128, length), jnp.float32),
            pltpu.VMEM((2 * length // 128, 128, length), jnp.float32),
            pltpu.VMEM((128, near.shape[-1]), jnp.float32),
        ],
        name="attend_back",
    )(query_rows, grad_rows, own, own, far, far, seg_row, seg_own, seg_far, near, beyond, log_totals)


def low(values):
    return values.astype(jnp.bfloat16)


def wide(values):
    return values.astype(jnp.float32)


def mul(first, second):
    return jnp.dot(first, second, preferred_element_type=jnp.float32)


def ein(spec, first, second):
    return jnp.einsum(spec, first, second, preferred_element_type=jnp.float32)


def quad():
    return lax.axis_size("shard") == 4 and lax.axis_size("ctx") == 2


def swap(values, axis, mask):
    return lax.ppermute(values, axis, [(i, i ^ mask) for i in range(lax.axis_size(axis))])


def spots():
    shard = lax.axis_index("shard")
    return shard // 2, shard % 2, lax.axis_index("ctx")


def pick(bit, values, axis):
    return lax.dynamic_index_in_dim(values, bit, axis, keepdims=False)


def ordered(bit, own, other, axis):
    return jnp.stack((jnp.where(bit == 0, own, other), jnp.where(bit == 0, other, own)), axis)


def gather_rows(block):
    if not quad():
        return lax.all_gather(block, ("shard", "ctx"), axis=0, tiled=True)
    far, core, side = spots()
    width = block.shape[1]
    if width % 256 == 0:
        half = width // 2
        left, right = block[:, :half], block[:, half:]
        left_pair = ordered(side, left, swap(left, "ctx", 1), 0)
        right_pair = ordered(far, right, swap(right, "shard", 2), 0)
        left_four = ordered(far, left_pair, swap(left_pair, "shard", 2), 0)
        right_four = ordered(side, right_pair, swap(right_pair, "ctx", 1), 1)
        four = jnp.concatenate((left_four, right_four), axis=-1)
    else:
        pair = ordered(side, block, swap(block, "ctx", 1), 0)
        four = ordered(far, pair, swap(pair, "shard", 2), 0)
    return ordered(core, four, swap(four, "shard", 1), 1).reshape(-1, width)


def added(axis, mask, bit, values, dim, kind=jnp.bfloat16):
    sent = pick(1 - bit, values, dim).astype(kind)
    return pick(bit, values, dim) + wide(swap(sent, axis, mask))


def scatter_rows(grads):
    if not quad():
        return lax.psum_scatter(grads, ("shard", "ctx"), scatter_dimension=0, tiled=True)
    far, core, side = spots()
    width = grads.shape[1]
    half = width // 2
    four = added("shard", 1, core, grads.reshape(2, 2, 2, -1, width), 1)
    left, right = four[..., :half], four[..., half:]
    left = added("shard", 2, far, left, 0)
    right = added("ctx", 1, side, right, 1)
    left = added("ctx", 1, side, left, 0)
    right = added("shard", 2, far, right, 0)
    return jnp.concatenate((left, right), axis=-1)


def scatter_small(blocks, shared_rows):
    if not quad():
        own = lax.psum_scatter(blocks, ("shard", "ctx"), scatter_dimension=0, tiled=True)[0]
        return own[:-shared_rows], own[-shared_rows:], lax.psum(own[:-shared_rows], "tp")
    far, core, side = spots()
    own = blocks.reshape((2, 2, 2) + blocks.shape[1:])
    own = added("shard", 1, core, own, 1, jnp.float32)
    own = added("shard", 2, far, own, 0, jnp.float32)
    own = added("ctx", 1, side, own, 0, jnp.float32)
    rows = own[:-shared_rows]
    tp_count = lax.axis_size("tp")
    step = 1
    while step < tp_count:
        rows = rows + swap(rows, "tp", step)
        step *= 2
    return None, own[-shared_rows:], rows


def spread_tp(chunk):
    count = lax.axis_size("tp")
    copies = jnp.broadcast_to(chunk[None], (count,) + chunk.shape)
    return lax.all_to_all(copies, "tp", split_axis=0, concat_axis=0, tiled=True)


def trade_tp(pieces):
    return lax.all_to_all(pieces, "tp", split_axis=0, concat_axis=0, tiled=True)


def gather_ctx(part):
    side = lax.axis_index("ctx")
    both = ordered(side, part, swap(part, "ctx", 1), 0)
    return both.reshape(-1, part.shape[1])


def scatter_ctx(grads):
    side = lax.axis_index("ctx")
    return added("ctx", 1, side, grads.reshape(2, -1, grads.shape[1]), 0)


def place_maps(routes, pair_order, experts, capacity):
    tok_rows = routes.shape[0]
    flat_route = routes.T.reshape(-1)
    flat_order = pair_order.T.reshape(-1)
    onehot = flat_route[None, :] == jnp.arange(experts, dtype=jnp.int32)[:, None]
    before = low(flat_order[:, None] < flat_order[None, :])
    earlier = mul(low(onehot), before)
    position = jnp.sum(jnp.where(onehot, earlier, 0.0), axis=0)
    slot = jnp.where(position < capacity, position, -1.0)
    split_hot = onehot.reshape(experts, 2, tok_rows)
    places = jnp.sum(jnp.where(split_hot, slot.reshape(1, 2, tok_rows) + 1.0, 0.0), axis=1) - 1.0
    others = jnp.sum(jnp.where(split_hot, wide(flat_route.reshape(1, 2, tok_rows)[:, ::-1]), 0.0), axis=1)
    return places, others


def hot_places(places, capacity):
    slots = jnp.arange(capacity, dtype=jnp.float32)
    return low(places[..., None, :] == slots[:, None])


def halved(places):
    count = lax.axis_size("tp")
    split = places.reshape(places.shape[:-1] + (count, HALVES, -1))
    moved = jnp.swapaxes(split, -3, -2)
    return moved.reshape(places.shape[:-1] + (HALVES, -1))


def all_shards(block):
    beyond = swap(block, "shard", 2)
    near = swap(jnp.stack((block, beyond)), "shard", 1)
    return block, near[0], beyond, near[1]


def norm_back(grads, scaled, inv_root, gain):
    slope = grads * gain
    return inv_root * (slope - scaled * jnp.mean(slope * scaled, axis=-1, keepdims=True))


def gelu_gate(gate_pre, up_pre):
    return jax.nn.gelu(gate_pre, approximate=True) * up_pre


def body(
    tokens, cotangent, segment_ids, routes, pair_order, rel_bucket, attn_gain, w_query, w_key, w_value, w_output,
    bias_table, ffn_gain, w_router, expert_gate, expert_up, expert_down,
):
    shard, side, part = lax.axis_index("shard"), lax.axis_index("ctx"), lax.axis_index("tp")
    shards, tp_count = lax.axis_size("shard"), lax.axis_size("tp")
    tok_rows, model_width = tokens.shape
    experts = w_router.shape[1]
    capacity = 9 * 2 * tok_rows // (8 * experts)
    local_width = w_query.shape[1]
    chunk_rows = tok_rows // tp_count
    four = quad()

    small_count = 2 + experts
    small_rows = -(-small_count // 8) * 8
    small = jnp.concatenate((attn_gain[None], ffn_gain[None], w_router.T), axis=0)
    small = jnp.pad(small, ((0, small_rows - small_count), (0, 0)))
    small_all = gather_rows(small).reshape(-1, small_rows, small.shape[1])
    small_all = jnp.swapaxes(small_all, 0, 1).reshape(small_rows, model_width)
    gain_attn, gain_ffn = wide(small_all[0]), wide(small_all[1])
    router_rows = small_all[2 : 2 + experts]
    joined_w = gather_rows(jnp.concatenate((w_query, w_key, w_value), axis=1))
    query_w, pair_w = joined_w[:, :local_width], joined_w[:, local_width:]
    output_block = jnp.moveaxis(spread_tp(w_output), 0, 1).reshape(w_output.shape[0], -1)
    output_w = gather_rows(output_block)

    places, others = place_maps(routes, pair_order, experts, capacity)
    route_maps = jnp.stack((places, others), axis=1)
    sent_maps = lax.all_to_all(route_maps, "shard", split_axis=0, concat_axis=0, tiled=True)
    if four:
        sent_maps = sent_maps[jnp.arange(shards) ^ shard]
    hot = hot_places(sent_maps[:, 0], capacity)
    other_slot = jnp.sum(jnp.where(hot > 0, sent_maps[:, 1][:, None, :], 0.0), axis=2).reshape(-1)
    if four:
        grad_rows = low(ein("sct,std->scd", hot, jnp.stack(all_shards(cotangent))))
    else:
        own_hot = hot_places(places, capacity)
        grad_rows = low(ein("ect,td->ecd", own_hot, cotangent))
        grad_rows = lax.all_to_all(grad_rows, "shard", split_axis=0, concat_axis=0, tiled=True)
    grad_rows = grad_rows.reshape(-1, model_width)

    gate_w, up_w, down_w = gather_ctx(expert_gate[0]), gather_ctx(expert_up[0]), gather_ctx(expert_down[0])

    rows_in = wide(tokens)
    root_one = lax.rsqrt(jnp.mean(rows_in * rows_in, axis=-1, keepdims=True) + EPSILON)
    normed = low(rows_in * root_one * gain_attn)
    own_pair = low(mul(normed, pair_w))
    far_pair = swap(own_pair, "ctx", 1)
    query_rows = low(low(ein("dh,td->ht", query_w, normed)) * 0.125)
    segments = segment_ids[0]
    seg_own = lax.dynamic_slice_in_dim(segments, side * tok_rows, tok_rows)
    seg_far = lax.dynamic_slice_in_dim(segments, (1 - side) * tok_rows, tok_rows)
    buckets = jnp.pad(rel_bucket, (1, 0), constant_values=-1)
    bucket_hot = low(buckets[:, None] == jnp.arange(bias_table.shape[0], dtype=jnp.int32)[None, :])
    near_hot = bucket_hot[tok_rows : 3 * tok_rows][::-1]
    beyond_hot = lax.dynamic_slice_in_dim(bucket_hot, 2 * tok_rows * (1 - side), 2 * tok_rows)[::-1]
    heads = bias_table.shape[1]
    near = ein("qb,bh->hq", near_hot, bias_table).reshape(heads // 2, 2, -1)
    beyond = ein("qb,bh->hq", beyond_hot, bias_table).reshape(heads // 2, 2, -1)
    masks = (seg_own[None, :], seg_own[:, None], seg_far[:, None], near, beyond)
    context, log_totals = attend(query_rows, own_pair, far_pair, *masks, tp_count)
    context_all = trade_tp(context).reshape(-1, chunk_rows)

    chunk_in = lax.dynamic_slice_in_dim(rows_in, part * chunk_rows, chunk_rows, 0)
    chunk_grad = wide(lax.dynamic_slice_in_dim(cotangent, part * chunk_rows, chunk_rows, 0))
    hidden = chunk_in + ein("ht,dh->td", context_all, output_w)
    root_two = lax.rsqrt(jnp.mean(hidden * hidden, axis=-1, keepdims=True) + EPSILON)
    scaled_two = hidden * root_two
    moe_in = low(scaled_two * gain_ffn)

    if four:
        hot_in = jnp.swapaxes(hot_places(halved(sent_maps[:, 0]), capacity), 0, 1)
        pieces = moe_in.reshape(HALVES, -1, model_width)
        expert_rows = None
        for half in range(HALVES):
            spread = spread_tp(pieces[half]).reshape(-1, model_width)
            more = ein("sct,std->scd", hot_in[half], jnp.stack(all_shards(spread)))
            expert_rows = more if expert_rows is None else expert_rows + more
        expert_rows = low(expert_rows)
    else:
        spread = spread_tp(moe_in).reshape(-1, model_width)
        expert_rows = low(ein("ect,td->ecd", own_hot, spread))
        expert_rows = lax.all_to_all(expert_rows, "shard", split_axis=0, concat_axis=0, tiled=True)
    expert_rows = expert_rows.reshape(-1, model_width)

    slot_logits = ein("sd,ed->se", expert_rows, router_rows)
    ids = jnp.arange(experts, dtype=jnp.float32)
    own_logit = jnp.sum(jnp.where(ids[None, :] == wide(shard), slot_logits, 0.0), axis=1)
    other_logit = jnp.sum(jnp.where(ids[None, :] == other_slot[:, None], slot_logits, 0.0), axis=1)
    slot_gate = jax.nn.softmax(jnp.stack((own_logit, other_logit), axis=1), axis=1)[:, :1]
    out_slope = mul(grad_rows, down_w)
    gate_pre = mul(expert_rows, gate_w)
    up_pre = mul(expert_rows, up_w)
    product, pull_gate = jax.vjp(gelu_gate, gate_pre, up_pre)
    activated = low(product)
    grad_act = wide(low(slot_gate * out_slope))
    grad_gate_pre, grad_up_pre = pull_gate(grad_act)
    grad_gate_low, grad_up_low = low(grad_gate_pre), low(grad_up_pre)
    gate_slopes = jnp.sum(out_slope * wide(activated), axis=1)
    weighted = low(slot_gate * wide(activated))
    grad_in = low(ein("sf,df->sd", grad_gate_low, gate_w) + ein("sf,df->sd", grad_up_low, up_w))
    expert_out = low(ein("sf,df->sd", weighted, down_w))

    def combine(slot_values):
        if not four:
            back = slot_values.reshape(shards, capacity, model_width)
            back = lax.all_to_all(back, "shard", split_axis=0, concat_axis=0, tiled=True)
            mixed = low(ein("ect,ecd->td", own_hot, back))
            return jnp.sum(wide(trade_tp(mixed.reshape(tp_count, chunk_rows, model_width))), axis=0)
        split = slot_values.reshape(shards, capacity, model_width)
        halves = []
        for half in range(HALVES):
            partial = ein("sct,scd->std", hot_in[half], split)
            received = swap(low(jnp.stack((partial[1], partial[3]))), "shard", 1)
            own = partial[0] + wide(received[0])
            beyond_part = low(partial[2] + wide(received[1]))
            own = low(own + wide(swap(beyond_part, "shard", 2)))
            moved = trade_tp(own.reshape(tp_count, -1, model_width))
            halves.append(jnp.sum(wide(moved), axis=0))
        return jnp.concatenate(halves, axis=0)

    grad_moe_in = combine(grad_in)
    token_slopes = jnp.sum(wide(hot) * gate_slopes.reshape(shards, capacity)[:, :, None], axis=1)
    if four:
        token_slopes = token_slopes[jnp.arange(shards) ^ shard]
    token_slopes = lax.all_to_all(token_slopes, "shard", split_axis=0, concat_axis=0, tiled=True)
    token_slopes = jnp.swapaxes(token_slopes.reshape(experts, tp_count, chunk_rows), 0, 1)
    token_slopes = jnp.sum(trade_tp(token_slopes), axis=0)

    chunk_routes = lax.dynamic_slice_in_dim(routes, part * chunk_rows, chunk_rows, 0)
    route_hot = chunk_routes[:, :, None] == jnp.arange(experts, dtype=jnp.int32)[None, None, :]
    logits = ein("td,ed->te", moe_in, router_rows)
    gate_values = jax.nn.softmax(jnp.sum(jnp.where(route_hot, logits[:, None, :], 0.0), axis=2), axis=1)
    grad_gates = jnp.sum(jnp.where(route_hot, token_slopes.T[:, None, :], 0.0), axis=2)
    grad_chosen = gate_values * (grad_gates - jnp.sum(gate_values * grad_gates, axis=1, keepdims=True))
    grad_logits = low(jnp.sum(jnp.where(route_hot, grad_chosen[:, :, None], 0.0), axis=1))
    grad_normed_two = grad_moe_in + ein("te,ed->td", grad_logits, router_rows)
    grad_hidden = chunk_grad + norm_back(grad_normed_two, scaled_two, root_two, gain_ffn)
    grad_branch = low(grad_hidden)
    grad_context = low(ein("td,dh->ht", grad_branch, output_w)).reshape(tp_count, -1, chunk_rows)
    grad_context = trade_tp(grad_context)
    router_part = ein("te,td->ed", grad_logits, moe_in)
    ffn_gain_part = jnp.sum(grad_normed_two * scaled_two, axis=0)

    layer_chunk = low(hidden + combine(expert_out))
    layer_out = spread_tp(layer_chunk).reshape(tok_rows, model_width)
    grad_gate_w = scatter_ctx(ein("sd,sf->df", expert_rows, grad_gate_low))
    grad_up_w = scatter_ctx(ein("sd,sf->df", expert_rows, grad_up_low))
    grad_down_w = scatter_ctx(ein("sd,sf->df", grad_rows, weighted))
    branch_all = spread_tp(grad_branch)
    grad_output_w = scatter_rows(ein("jtd,jht->dh", branch_all, context))

    query_grad, key_own, value_own, key_far, value_far, bands = attend_back(
        query_rows, grad_context, own_pair, far_pair, *masks, log_totals
    )
    received = swap(jnp.concatenate((key_far, value_far), axis=1), "ctx", 1)
    pair_grad = low(jnp.concatenate((key_own, value_own), axis=1) + wide(received))
    grad_normed = ein("ht,dh->td", query_grad, query_w) + ein("th,dh->td", pair_grad, pair_w)
    scaled_one = rows_in * root_one
    attn_gain_part = jnp.sum(grad_normed * scaled_one, axis=0)
    moved = trade_tp(low(grad_normed).reshape(tp_count, chunk_rows, model_width))
    chunk_normed = jnp.sum(wide(moved), axis=0)
    chunk_scaled = lax.dynamic_slice_in_dim(scaled_one, part * chunk_rows, chunk_rows, 0)
    chunk_root = lax.dynamic_slice_in_dim(root_one, part * chunk_rows, chunk_rows, 0)
    chunk_tokens = grad_hidden + norm_back(chunk_normed, chunk_scaled, chunk_root, gain_attn)
    tokens_grad = wide(spread_tp(low(chunk_tokens)).reshape(tok_rows, model_width))
    grad_joined = jnp.concatenate(
        (ein("td,ht->dh", normed, query_grad), ein("td,th->dh", normed, pair_grad)), axis=1
    )
    grad_joined = scatter_rows(grad_joined)

    bands = bands.reshape(heads // 2, 2, 2, -1)
    near_band = bands[:, 0].reshape(heads, -1)
    far_band = bands[:, 1].reshape(heads, -1)
    table_part = jnp.dot(wide(near_hot).T, near_band.T, precision=HIGHEST_PRECISION) + jnp.dot(
        wide(beyond_hot).T, far_band.T, precision=HIGHEST_PRECISION
    )
    owner_rows = attn_gain.shape[0]
    owners = model_width // owner_rows
    rows = jnp.concatenate((attn_gain_part[None], ffn_gain_part[None], router_part), axis=0)
    rows = jnp.swapaxes(rows.reshape(small_count, owners, owner_rows), 0, 1)
    table_rows = table_part.reshape(1, -1, owner_rows)
    shared_rows = table_rows.shape[1]
    table_rows = jnp.broadcast_to(table_rows, (owners, shared_rows, owner_rows))
    _, table_sum, small_sum = scatter_small(jnp.concatenate((rows, table_rows), axis=1), shared_rows)
    return (
        layer_out,
        tokens_grad,
        small_sum[0],
        grad_joined[:, :local_width],
        grad_joined[:, local_width : 2 * local_width],
        grad_joined[:, 2 * local_width :],
        grad_output_w,
        table_sum.reshape(bias_table.shape),
        small_sum[1],
        small_sum[2:].T,
        grad_gate_w[None],
        grad_up_w[None],
        grad_down_w[None],
    )


def solution(mesh):
    return jax.shard_map(
        body,
        mesh=mesh,
        in_specs=(
            P(("shard", "ctx"), None),
            P(("shard", "ctx"), None),
            P("shard", None),
            P(("shard", "ctx"), None),
            P(("shard", "ctx"), None),
            P(),
            P(("shard", "ctx")),
            P(("shard", "ctx"), "tp"),
            P(("shard", "ctx"), "tp"),
            P(("shard", "ctx"), "tp"),
            P(("shard", "ctx"), "tp"),
            P(None, "tp"),
            P(("shard", "ctx")),
            P(("shard", "ctx"), None),
            P("shard", "ctx", "tp"),
            P("shard", "ctx", "tp"),
            P("shard", "ctx", "tp"),
        ),
        out_specs=(
            P(("shard", "ctx"), None),
            P(("shard", "ctx"), None),
            P(("shard", "ctx")),
            P(("shard", "ctx"), "tp"),
            P(("shard", "ctx"), "tp"),
            P(("shard", "ctx"), "tp"),
            P(("shard", "ctx"), "tp"),
            P(None, "tp"),
            P(("shard", "ctx")),
            P(("shard", "ctx"), None),
            P("shard", "ctx", "tp"),
            P("shard", "ctx", "tp"),
            P("shard", "ctx", "tp"),
        ),
        check_vma=False,
    )
```

```python
import functools

import jax
import jax.numpy as jnp
from jax import lax
from jax.experimental import pallas as pl
from jax.experimental.pallas import tpu as pltpu
from jax.sharding import PartitionSpec as P


HEAD_DIM = 64
EPSILON = 1e-06
NEGATIVE = -1e30
HIGHEST_PRECISION = lax.Precision.HIGHEST
GELU_SCALE = 0.7978845608028654
GELU_CUBE = 0.044715
BACK_GROUPS = (1, 1, 2)
LAYER_GROUPS = (2, 2)
SHARD, CTX, TP = "shard", "ctx", "tp"
EXTRA = 16


def toeplitz(window_row, rows, width):
    spread = jnp.broadcast_to(window_row, (rows, window_row.shape[1]))
    turned = pltpu.roll(spread, width - rows + 1, 1, stride=1, stride_axis=0)
    return turned


def attend_kernel(query_ref, key_own, value_own, key_far, value_far, seg_row, seg_own, seg_far, near_ref, far_ref, out_ref, total_ref, bias, kept):
    rows = 128
    length = key_own.shape[0]
    blocks = length // rows
    width = near_ref.shape[-1]
    across = (((1,), (1,)), ((), ()))
    for head in range(2):
        lanes = slice(head * HEAD_DIM, (head + 1) * HEAD_DIM)
        query = query_ref[:, lanes]
        bias[0] = toeplitz(near_ref[0, head : head + 1, :], rows, width)
        bias[1] = toeplitz(far_ref[0, head : head + 1, :], rows, width)
        highest = None
        for part in range(2):
            keys, segs = ((key_own, seg_own), (key_far, seg_far))[part]
            for block in range(blocks):
                span = slice(block * rows, (block + 1) * rows)
                first = (blocks - 1 - block) * rows
                scores = lax.dot_general(keys[span, lanes], query, across, preferred_element_type=jnp.float32)
                scores = scores + bias[part, :, first : first + length]
                scores = jnp.where(segs[span, :] == seg_row[...], scores, NEGATIVE)
                kept[part * blocks + block] = scores
                top = jnp.max(scores, axis=0, keepdims=True)
                highest = top if highest is None else jnp.maximum(highest, top)
        total = None
        context = None
        for part in range(2):
            vals = (value_own, value_far)[part]
            for block in range(blocks):
                span = slice(block * rows, (block + 1) * rows)
                grown = jnp.exp(kept[part * blocks + block] - highest)
                added = jnp.sum(grown, axis=0, keepdims=True)
                total = added if total is None else total + added
                more = lax.dot_general(
                    vals[span, lanes], grown.astype(jnp.bfloat16), (((0,), (0,)), ((), ())),
                    preferred_element_type=jnp.float32,
                )
                context = more if context is None else context + more
        out_ref[:, lanes] = (context / total).T.astype(jnp.bfloat16)
        total_ref[0, head : head + 1, :] = highest + jnp.log(total)


def attend_back_kernel(query_ref, grad_ref, key_own, value_own, key_far, value_far, seg_row, seg_own, seg_far, near_ref, far_ref, total_ref,
                       grad_query, pair_own, pair_far, band_ref, bias, kept, slopes, gathered):
    rows = 128
    length = key_own.shape[0]
    blocks = length // rows
    width = near_ref.shape[-1]
    across = (((1,), (1,)), ((), ()))
    down = (((0,), (0,)), ((), ()))
    for head in range(2):
        lanes = slice(head * HEAD_DIM, (head + 1) * HEAD_DIM)
        query = query_ref[:, lanes]
        grads = grad_ref[:, lanes]
        log_total = total_ref[0, head : head + 1, :]
        bias[0] = toeplitz(near_ref[0, head : head + 1, :], rows, width)
        bias[1] = toeplitz(far_ref[0, head : head + 1, :], rows, width)
        shared = None
        for part in range(2):
            keys, vals, segs, value_grad = (
                (key_own, value_own, seg_own, pair_own), (key_far, value_far, seg_far, pair_far),
            )[part]
            for block in range(blocks):
                span = slice(block * rows, (block + 1) * rows)
                first = (blocks - 1 - block) * rows
                scores = lax.dot_general(keys[span, lanes], query, across, preferred_element_type=jnp.float32)
                scores = scores + bias[part, :, first : first + length]
                scores = jnp.where(segs[span, :] == seg_row[...], scores, NEGATIVE)
                probs = jnp.exp(scores - log_total)
                slope = lax.dot_general(vals[span, lanes], grads, across, preferred_element_type=jnp.float32)
                value_grad[1, span, lanes] = jnp.dot(
                    probs.astype(jnp.bfloat16), grads, preferred_element_type=jnp.float32
                ).astype(value_grad.dtype)
                kept[part * blocks + block] = probs
                slopes[part * blocks + block] = slope
                added = jnp.sum(probs * slope, axis=0, keepdims=True)
                shared = added if shared is None else shared + added
        query_grad = None
        for part in range(2):
            keys, key_grad = ((key_own, pair_own), (key_far, pair_far))[part]
            gathered[...] = jnp.zeros_like(gathered)
            for block in range(blocks):
                span = slice(block * rows, (block + 1) * rows)
                first = (blocks - 1 - block) * rows
                change = kept[part * blocks + block] * (slopes[part * blocks + block] - shared)
                gathered[:, first : first + length] += change
                low = change.astype(jnp.bfloat16)
                key_grad[0, span, lanes] = jnp.dot(low, query, preferred_element_type=jnp.float32).astype(key_grad.dtype)
                more = lax.dot_general(keys[span, lanes], low, down, preferred_element_type=jnp.float32)
                query_grad = more if query_grad is None else query_grad + more
            flip = (
                lax.broadcasted_iota(jnp.int32, (rows, rows), 0) + lax.broadcasted_iota(jnp.int32, (rows, rows), 1) == rows - 1
            ).astype(jnp.float32)
            turned = jnp.dot(flip, gathered[...], precision=HIGHEST_PRECISION, preferred_element_type=jnp.float32)
            turned = pltpu.roll(turned, 0, 1, stride=1, stride_axis=0)
            band_ref[0, 2 * part + head : 2 * part + head + 1, :] = jnp.sum(turned, axis=0, keepdims=True)
        grad_query[:, lanes] = (query_grad * 0.125).T.astype(jnp.bfloat16)


def whole(array):
    zeros = (0,) * array.ndim
    return pl.BlockSpec(array.shape, lambda pair: zeros)


def attend(query_rows, pair, far, seg_row, seg_own, seg_far, near, beyond):
    length, features = query_rows.shape
    pairs = features // 128
    keys = pl.BlockSpec((length, 128), lambda pair: (0, pair))
    vals = pl.BlockSpec((length, 128), lambda pair: (0, pairs + pair))
    window = pl.BlockSpec((1, 2, near.shape[-1]), lambda pair: (pair, 0, 0))
    return pl.pallas_call(
        attend_kernel,
        grid=(pairs,),
        in_specs=[keys, keys, vals, keys, vals, whole(seg_row), whole(seg_own), whole(seg_far), window, window],
        out_specs=[keys, pl.BlockSpec((1, 2, length), lambda pair: (pair, 0, 0))],
        out_shape=[
            jax.ShapeDtypeStruct((length, features), jnp.bfloat16),
            jax.ShapeDtypeStruct((pairs, 2, length), jnp.float32),
        ],
        scratch_shapes=[
            pltpu.VMEM((2, 128, near.shape[-1]), jnp.float32),
            pltpu.VMEM((2 * length // 128, 128, length), jnp.float32),
        ],
        name="attend",
    )(query_rows, pair, pair, far, far, seg_row, seg_own, seg_far, near, beyond)


def attend_back(query_rows, grad_rows, pair, far, seg_row, seg_own, seg_far, near, beyond, log_totals):
    length, features = query_rows.shape
    pairs = features // 128
    keys = pl.BlockSpec((length, 128), lambda pair: (0, pair))
    vals = pl.BlockSpec((length, 128), lambda pair: (0, pairs + pair))
    window = pl.BlockSpec((1, 2, near.shape[-1]), lambda pair: (pair, 0, 0))
    both = pl.BlockSpec((2, length, 128), lambda pair: (0, 0, pair))
    tall = lambda kind: jax.ShapeDtypeStruct((2, length, features), kind)
    return pl.pallas_call(
        attend_back_kernel,
        grid=(pairs,),
        in_specs=[keys, keys, keys, vals, keys, vals, whole(seg_row), whole(seg_own), whole(seg_far), window, window,
                  pl.BlockSpec((1, 2, length), lambda pair: (pair, 0, 0))],
        out_specs=[keys, both, both, pl.BlockSpec((1, 4, near.shape[-1]), lambda pair: (pair, 0, 0))],
        out_shape=[
            jax.ShapeDtypeStruct((length, features), jnp.bfloat16), tall(jnp.float32), tall(jnp.bfloat16),
            jax.ShapeDtypeStruct((pairs, 4, near.shape[-1]), jnp.float32),
        ],
        scratch_shapes=[
            pltpu.VMEM((2, 128, near.shape[-1]), jnp.float32),
            pltpu.VMEM((2 * length // 128, 128, length), jnp.float32),
            pltpu.VMEM((2 * length // 128, 128, length), jnp.float32),
            pltpu.VMEM((128, near.shape[-1]), jnp.float32),
        ],
        name="attend_back",
    )(query_rows, grad_rows, pair, pair, far, far, seg_row, seg_own, seg_far, near, beyond, log_totals)


TURN = (((0,), (0,)), ((), ()))
ACROSS = (((1,), (1,)), ((), ()))


def hot_of(row, slots):
    ids = lax.broadcasted_iota(jnp.int32, (slots, row.shape[1]), 0).astype(jnp.float32)
    return (ids == row).astype(jnp.bfloat16)


def fill_halves(side_ref, own_ref, far_ref, full_ref):
    half = own_ref.shape[1]
    side = side_ref[0]
    full_ref[:, pl.ds(pl.multiple_of(side * half, half), half)] = own_ref[...]
    full_ref[:, pl.ds(pl.multiple_of((1 - side) * half, half), half)] = far_ref[...]


def fold_into(hots, values, outs, groups, rows_sums=None, place=None):
    homes = [(group, index) for group, size in enumerate(groups) for index in range(size)]
    for piece, hot in enumerate(hots):
        folded = lax.dot_general(hot, values, TURN, preferred_element_type=jnp.float32)
        rows = folded.shape[0]
        more = 0 if rows_sums is None else EXTRA
        first = homes[piece][1] * (rows + more)
        out = outs[homes[piece][0]]
        out[0, first : first + rows, :] = folded.astype(jnp.bfloat16)
        if more:
            top = lax.broadcasted_iota(jnp.int32, (EXTRA, rows), 0) == 0
            out[0, first + rows : first + rows + EXTRA, :] = jnp.zeros((EXTRA, out.shape[2]), jnp.bfloat16)
            spread = jnp.where(top, rows_sums[piece], 0.0).astype(jnp.bfloat16)
            out[0, first + rows : first + rows + EXTRA, pl.ds(pl.multiple_of(place * rows, rows), rows)] = spread


def packed(groups, rows, sources, width):
    specs, shapes = [], []
    for size in groups + groups:
        specs.append(pl.BlockSpec((1, size * rows, width), lambda step, *_: (step // 2, 0, 0)))
        shapes.append(jax.ShapeDtypeStruct((sources // 2, size * rows, width), jnp.bfloat16))
    return specs, shapes


def slope_kernel(side_ref, places_ref, own_ref, far_ref, *refs):
    sources = len(refs) - 3
    rows_ref, slope_ref, full_ref = refs[sources:]
    source = pl.program_id(0)

    @pl.when(source == 0)
    def _():
        fill_halves(side_ref, own_ref, far_ref, full_ref)

    hot = hot_of(places_ref[0], rows_ref.shape[0])
    for index in range(sources):

        @pl.when(source == index)
        def _(block=refs[index]):
            rows_ref[...] = jnp.dot(hot, block[...], preferred_element_type=jnp.float32).astype(jnp.bfloat16)

    slope_ref[...] = lax.dot_general(rows_ref[...], full_ref[...], ACROSS, preferred_element_type=jnp.float32)


def fixed(array):
    zeros = (0,) * array.ndim
    return pl.BlockSpec(array.shape, lambda step, *_: zeros)


def slopes(side, places, down_own, down_far, blocks, slots):
    sources = places.shape[0]
    width, hidden = blocks[0].shape[1], down_own.shape[0]
    return pl.pallas_call(
        slope_kernel,
        grid_spec=pltpu.PrefetchScalarGridSpec(
            num_scalar_prefetch=1,
            grid=(sources,),
            in_specs=[pl.BlockSpec((1, 1, places.shape[1]), lambda step, *_: (step, 0, 0)), fixed(down_own), fixed(down_far)]
            + [fixed(block) for block in blocks],
            out_specs=[
                pl.BlockSpec((slots, width), lambda step, *_: (step, 0)),
                pl.BlockSpec((slots, hidden), lambda step, *_: (step, 0)),
            ],
            scratch_shapes=[pltpu.VMEM((hidden, width), jnp.bfloat16)],
        ),
        out_shape=[
            jax.ShapeDtypeStruct((sources * slots, width), jnp.bfloat16),
            jax.ShapeDtypeStruct((sources * slots, hidden), jnp.float32),
        ],
        name="slopes",
    )(side, places[:, None, :], down_own, down_far, *blocks)


def expert_kernel(groups, side_ref, places_ref, other_ref, own_ref, router_ref, gate_own, gate_far, up_own, up_far, slope_ref, *refs):
    many = len(groups)
    count = len(refs) - 4 - 2 * many - 2
    pieces = places_ref.shape[1]
    blocks, refs = refs[:count], refs[count:]
    rows_ref, gate_out, up_out, weighted_out = refs[:4]
    sent, kept = refs[4 : 4 + many], refs[4 + many : 4 + 2 * many]
    gate_full, up_full = refs[4 + 2 * many :]
    slots, width = rows_ref.shape
    source = pl.program_id(0)

    @pl.when(source == 0)
    def _():
        fill_halves(side_ref, gate_own, gate_far, gate_full)
        fill_halves(side_ref, up_own, up_far, up_full)

    hots = [hot_of(places_ref[0, piece : piece + 1, :], slots) for piece in range(pieces)]
    total_sources = count // pieces
    for index in range(total_sources):

        @pl.when(source == index)
        def _(index=index):
            for first in range(0, width, 256):
                total = None
                for piece in range(pieces):
                    block = blocks[piece * total_sources + index][:, first : first + 256]
                    more = jnp.dot(hots[piece], block, preferred_element_type=jnp.float32)
                    total = more if total is None else total + more
                rows_ref[:, first : first + 256] = total.astype(jnp.bfloat16)

    rows = rows_ref[...]
    logits = lax.dot_general(rows, router_ref[...], ACROSS, preferred_element_type=jnp.float32)
    ids = lax.broadcasted_iota(jnp.int32, logits.shape, 1).astype(jnp.float32)
    own = jnp.sum(logits * own_ref[...], axis=1, keepdims=True)
    other = jnp.sum(jnp.where(ids == other_ref[...], logits, 0.0), axis=1, keepdims=True)
    top = jnp.maximum(own, other)
    own, other = jnp.exp(own - top), jnp.exp(other - top)
    part = own / (own + other)
    sums = []
    step = slots // 3
    for first in range(0, slots, step):
        span = slice(first, first + step)
        gate = lax.dot_general(rows[span, :], gate_full[...], ACROSS, preferred_element_type=jnp.float32)
        up = lax.dot_general(rows[span, :], up_full[...], ACROSS, preferred_element_type=jnp.float32)
        slope = slope_ref[span, :]
        square = gate * gate
        bent = jnp.tanh(gate * (GELU_SCALE + (GELU_SCALE * GELU_CUBE) * square))
        half = 0.5 + 0.5 * bent
        curve = gate * half
        steep = half + curve * (1.0 - bent) * (GELU_SCALE + (3.0 * GELU_SCALE * GELU_CUBE) * square)
        act = curve * up
        back = part[span, :] * slope
        gate_out[span, :] = (back * up * steep).astype(jnp.bfloat16)
        up_out[span, :] = (back * curve).astype(jnp.bfloat16)
        weighted_out[span, :] = (part[span, :] * act).astype(jnp.bfloat16)
        sums.append(jnp.sum(slope * act, axis=1, keepdims=True))
    gathered = jnp.concatenate(sums, axis=0)
    rows_sums = [jnp.sum(hot.astype(jnp.float32) * gathered, axis=0, keepdims=True) for hot in hots]
    grads = jnp.dot(gate_out[...], gate_full[...], preferred_element_type=jnp.float32)
    grads = grads + jnp.dot(up_out[...], up_full[...], preferred_element_type=jnp.float32)
    low_grads = grads.astype(jnp.bfloat16)

    @pl.when(source % 2 == 1)
    def _():
        fold_into(hots, low_grads, sent, groups, rows_sums, side_ref[1])

    @pl.when(source % 2 == 0)
    def _():
        fold_into(hots, low_grads, kept, groups, rows_sums, side_ref[1])


def expert(side, places, other, own_hot, router, gates, ups, slope, blocks, groups):
    sources, pieces, chunk = places.shape
    slots = slope.shape[0] // sources
    hidden = slope.shape[1]
    flat = [block for piece in blocks for block in piece]
    width = flat[0].shape[1]
    rows = lambda columns: pl.BlockSpec((slots, columns), lambda step, *_: (step, 0))
    tall = lambda columns: jax.ShapeDtypeStruct((sources * slots, columns), jnp.bfloat16)
    packs, pair = packed(groups, chunk + EXTRA, sources, width)
    results = pl.pallas_call(
        functools.partial(expert_kernel, groups),
        grid_spec=pltpu.PrefetchScalarGridSpec(
            num_scalar_prefetch=1,
            grid=(sources,),
            in_specs=[
                pl.BlockSpec((1, pieces, chunk), lambda step, *_: (step, 0, 0)),
                pl.BlockSpec((slots, 1), lambda step, *_: (step, 0)),
                fixed(own_hot), fixed(router), fixed(gates[0]), fixed(gates[1]), fixed(ups[0]), fixed(ups[1]),
                rows(hidden),
            ]
            + [fixed(block) for block in flat],
            out_specs=[rows(width), rows(hidden), rows(hidden), rows(hidden)] + packs,
            scratch_shapes=[
                pltpu.VMEM((hidden, width), jnp.bfloat16), pltpu.VMEM((hidden, width), jnp.bfloat16),
            ],
        ),
        out_shape=[tall(width), tall(hidden), tall(hidden), tall(hidden)] + pair,
        name="expert",
    )(side, places, other, own_hot, router, gates[0], gates[1], ups[0], ups[1], slope, *flat)
    return results[:4], results[4 : 4 + len(groups)], results[4 + len(groups) :]


def output_kernel(groups, side_ref, places_ref, weighted_ref, own_ref, far_ref, *refs):
    many = len(groups)
    sent, kept, full_ref = refs[:many], refs[many : 2 * many], refs[-1]
    source = pl.program_id(0)

    @pl.when(source == 0)
    def _():
        fill_halves(side_ref, own_ref, far_ref, full_ref)

    hots = [hot_of(places_ref[0, piece : piece + 1, :], weighted_ref.shape[0]) for piece in range(places_ref.shape[1])]
    values = jnp.dot(weighted_ref[...], full_ref[...], preferred_element_type=jnp.float32)
    values = values.astype(jnp.bfloat16)

    @pl.when(source % 2 == 1)
    def _():
        fold_into(hots, values, sent, groups)

    @pl.when(source % 2 == 0)
    def _():
        fold_into(hots, values, kept, groups)


def outputs(side, places, weighted, down_own, down_far, groups):
    sources, pieces, chunk = places.shape
    slots, hidden = weighted.shape[0] // sources, weighted.shape[1]
    width = 2 * down_own.shape[1]
    packs, pair = packed(groups, chunk, sources, width)
    results = pl.pallas_call(
        functools.partial(output_kernel, groups),
        grid_spec=pltpu.PrefetchScalarGridSpec(
            num_scalar_prefetch=1,
            grid=(sources,),
            in_specs=[
                pl.BlockSpec((1, pieces, chunk), lambda step, *_: (step, 0, 0)),
                pl.BlockSpec((slots, hidden), lambda step, *_: (step, 0)),
                fixed(down_own), fixed(down_far),
            ],
            out_specs=packs,
            scratch_shapes=[pltpu.VMEM((hidden, width), jnp.bfloat16)],
        ),
        out_shape=pair,
        name="outputs",
    )(side, places, weighted, down_own, down_far)
    return results[: len(groups)], results[len(groups) :]


def weight_kernel(side_ref, rows_ref, grads_ref, gate_ref, up_ref, weighted_ref, *outs):
    half = outs[0].shape[1]
    own = pl.ds(pl.multiple_of(side_ref[0] * half, half), half)
    far = pl.ds(pl.multiple_of((1 - side_ref[0]) * half, half), half)
    for index, (left, right) in enumerate(((gate_ref, rows_ref), (up_ref, rows_ref), (weighted_ref, grads_ref))):
        for span, out in ((far, outs[index]), (own, outs[3 + index])):
            total = lax.dot_general(left[...], right[:, span], TURN, preferred_element_type=jnp.float32)
            out[...] = total.astype(out.dtype)


def weight_grads(side, rows, grads, gate, up, weighted):
    hidden, half = gate.shape[1], rows.shape[1] // 2
    kinds = [jnp.bfloat16] * 3 + [jnp.float32] * 3
    inputs = (rows, grads, gate, up, weighted)
    results = pl.pallas_call(
        weight_kernel,
        grid_spec=pltpu.PrefetchScalarGridSpec(
            num_scalar_prefetch=1,
            grid=(1,),
            in_specs=[fixed(block) for block in inputs],
            out_specs=[pl.BlockSpec((hidden, half), lambda *_: (0, 0))] * 6,
        ),
        out_shape=[jax.ShapeDtypeStruct((hidden, half), kind) for kind in kinds],
        name="weights",
    )(side, *inputs)
    return results[:3], results[3:]


def rows_kernel(spot_ref, left_ref, right_ref, *refs):
    sent_ref, kept_ref = refs[-2:]
    columns = right_ref.shape[1]
    rows = sent_ref.shape[2]
    total = lax.dot_general(left_ref[...], right_ref[...], TURN, preferred_element_type=jnp.float32).astype(jnp.bfloat16)

    def store(out_ref):
        for side in range(2):
            span = slice(side * rows, (side + 1) * rows)
            out_ref[0, side, :, :columns] = total[span, :]
            if len(refs) > 2:
                out_ref[0, side, :, columns:] = refs[0][span, :].astype(jnp.bfloat16)

    @pl.when(pl.program_id(0) == 0)
    def _():
        store(sent_ref)

    @pl.when(pl.program_id(0) == 1)
    def _():
        store(kept_ref)


def row_grads(core, left, right, *small):
    width, columns = left.shape[1], right.shape[1]
    rows = width // 8
    block = lambda kept, far, spot: far * 2 + (spot[0] ^ (1 - kept))
    total = columns + sum(more.shape[1] for more in small)
    return pl.pallas_call(
        rows_kernel,
        grid_spec=pltpu.PrefetchScalarGridSpec(
            num_scalar_prefetch=1,
            grid=(2, 2),
            in_specs=[
                pl.BlockSpec((left.shape[0], 2 * rows), lambda *at: (0, block(*at))),
                pl.BlockSpec(right.shape, lambda *_: (0, 0)),
            ]
            + [pl.BlockSpec((2 * rows, more.shape[1]), lambda *at: (block(*at), 0)) for more in small],
            out_specs=[
                pl.BlockSpec((1, 2, rows, total), lambda kept, far, spot: (jnp.where(kept == 0, far, 1), 0, 0, 0)),
                pl.BlockSpec((1, 2, rows, total), lambda kept, far, spot: (jnp.where(kept == 0, 0, far), 0, 0, 0)),
            ],
        ),
        out_shape=[jax.ShapeDtypeStruct((2, 2, rows, total), jnp.bfloat16)] * 2,
        name="row_grads",
    )(core[None], left, right, *small)


LEFT = (((0, 0, 0), (0, 0, 1)), ((1, 0, 0), (1, 0, 1)), ((0, 1, 0), (0, 1, 1)), ((1, 1, 0), (1, 1, 1)))
RIGHT = (((0, 0, 0), (1, 0, 0)), ((0, 0, 1), (1, 0, 1)), ((0, 1, 0), (1, 1, 0)), ((0, 1, 1), (1, 1, 1)))


def lay_out(spot_ref, parts, out_ref, pieces, small_ref=None):
    half = out_ref.shape[1] // 2
    columns = half // pieces
    rows = out_ref.shape[0] // 8
    for side, where in enumerate((LEFT, RIGHT)):
        for index, offsets in enumerate(where):
            part = parts[4 * side + index]
            high = part.shape[0] // 2
            for number, (far, core, ctx) in enumerate(offsets):
                block = ((spot_ref[0] ^ far) * 2 + (spot_ref[1] ^ core)) * 2 + (spot_ref[2] ^ ctx)
                span = pl.ds(pl.multiple_of(block * rows, rows), rows)
                for piece in range(pieces):
                    values = part[number * high : number * high + rows, piece * columns : (piece + 1) * columns]
                    if pieces == 1:
                        out_ref[span, side * half : (side + 1) * half] = values
                    else:
                        target = spot_ref[3] ^ (side * pieces + piece)
                        out_ref[span, pl.ds(pl.multiple_of(target * columns, columns), columns)] = values
                if high > rows:
                    small_ref[:, span] = part[number * high + rows : (number + 1) * high, :rows]


def project_kernel(spot_ref, tokens_ref, *refs):
    query_ref, pair_ref, joined_ref, normed_ref, small_ref = refs[-5:]
    lay_out(spot_ref, refs[:-5], joined_ref, 1, small_ref)
    rows = tokens_ref[...].astype(jnp.float32)
    root = lax.rsqrt(jnp.mean(rows * rows, axis=-1, keepdims=True) + EPSILON)
    gain = small_ref[...].astype(jnp.float32)[:1, :]
    normed_ref[...] = (rows * root * gain).astype(jnp.bfloat16)
    split = query_ref.shape[1]
    result = jnp.dot(normed_ref[...], joined_ref[...], preferred_element_type=jnp.float32).astype(jnp.bfloat16)
    query_ref[...] = (result[:, :split].astype(jnp.float32) * 0.125).astype(jnp.bfloat16)
    pair_ref[...] = result[:, split:]


def project(spot, tokens, parts):
    rows, width = tokens.shape
    columns = parts[0].shape[1] * 2
    extra = parts[0].shape[0] // 2 - width // 8
    shapes = [(rows, columns // 3), (rows, 2 * columns // 3), (width, columns), (rows, width), (extra, width)]
    return pl.pallas_call(
        project_kernel,
        grid_spec=pltpu.PrefetchScalarGridSpec(
            num_scalar_prefetch=1,
            grid=(1,),
            in_specs=[fixed(tokens)] + [fixed(part) for part in parts],
            out_specs=[pl.BlockSpec(shape, lambda *_: (0, 0)) for shape in shapes],
        ),
        out_shape=[jax.ShapeDtypeStruct(shape, jnp.bfloat16) for shape in shapes],
        name="project",
    )(spot, tokens, *parts)


def lay_kernel(pieces, spot_ref, *refs):
    lay_out(spot_ref, refs[:-1], refs[-1], pieces)


def laid(spot, parts, width, pieces):
    columns = parts[0].shape[1] * 2
    return pl.pallas_call(
        functools.partial(lay_kernel, pieces),
        grid_spec=pltpu.PrefetchScalarGridSpec(
            num_scalar_prefetch=1,
            grid=(1,),
            in_specs=[fixed(part) for part in parts],
            out_specs=pl.BlockSpec((width, columns), lambda *_: (0, 0)),
        ),
        out_shape=jax.ShapeDtypeStruct((width, columns), jnp.bfloat16),
        name="laid",
    )(spot, *parts)


def join_kernel(part_ref, *refs):
    out_ref = refs[-1]
    for step, piece in enumerate(refs[:-1]):
        rows = piece.shape[0]
        target = part_ref[0] ^ step
        out_ref[pl.ds(pl.multiple_of(target * rows, rows), rows), :] = piece[...].astype(out_ref.dtype)


def join_rows(part, pieces, kind):
    shape = (len(pieces) * pieces[0].shape[0], pieces[0].shape[1])
    return pl.pallas_call(
        join_kernel,
        grid_spec=pltpu.PrefetchScalarGridSpec(
            num_scalar_prefetch=1,
            grid=(1,),
            in_specs=[fixed(piece) for piece in pieces],
            out_specs=pl.BlockSpec(shape, lambda *_: (0, 0)),
        ),
        out_shape=jax.ShapeDtypeStruct(shape, kind),
        name="join_rows",
    )(part[None], *pieces)


def low(values):
    return values.astype(jnp.bfloat16)


def wide(values):
    return values.astype(jnp.float32)


def mul(first, second):
    return jnp.dot(first, second, preferred_element_type=jnp.float32)


def ein(spec, first, second):
    return jnp.einsum(spec, first, second, preferred_element_type=jnp.float32)


def quad():
    return lax.axis_size(SHARD) == 4 and lax.axis_size(CTX) == 2


def swap(values, axis, mask):
    return lax.ppermute(values, axis, [(i, i ^ mask) for i in range(lax.axis_size(axis))])


def spots():
    shard = lax.axis_index(SHARD)
    return shard // 2, shard % 2, lax.axis_index(CTX)


def pick(bit, values, axis):
    return lax.dynamic_index_in_dim(values, bit, axis, keepdims=False)


def ordered(bit, own, other, axis):
    return jnp.stack((jnp.where(bit == 0, own, other), jnp.where(bit == 0, other, own)), axis)


def gather_rows(block):
    if not quad():
        return lax.all_gather(block, (SHARD, CTX), axis=0, tiled=True)
    far, core, side = spots()
    width = block.shape[1]
    if width % 256 == 0:
        half = width // 2
        left, right = block[:, :half], block[:, half:]
        left_pair = ordered(side, left, swap(left, CTX, 1), 0)
        right_pair = ordered(far, right, swap(right, SHARD, 2), 0)
        left_four = ordered(far, left_pair, swap(left_pair, SHARD, 2), 0)
        right_four = ordered(side, right_pair, swap(right_pair, CTX, 1), 1)
        four = jnp.concatenate((left_four, right_four), axis=-1)
    else:
        pair = ordered(side, block, swap(block, CTX, 1), 0)
        four = ordered(far, pair, swap(pair, SHARD, 2), 0)
    return ordered(core, four, swap(four, SHARD, 1), 1).reshape(-1, width)


def stage_one(left, right):
    left = jnp.concatenate((left, swap(left, CTX, 1)), axis=0)
    return left, jnp.concatenate((right, swap(right, SHARD, 2)), axis=0)


def stage_two(left, right):
    return swap(left, SHARD, 2), swap(right, CTX, 1)


def stage_three(pair, more):
    parts = (pair[0], more[0], pair[1], more[1])
    far = [swap(part, SHARD, 1) for part in parts]
    return [parts[0], parts[1], far[0], far[1], parts[2], parts[3], far[2], far[3]]


def added(axis, mask, bit, values, dim, kind=jnp.bfloat16):
    sent = pick(1 - bit, values, dim).astype(kind)
    return pick(bit, values, dim) + wide(swap(sent, axis, mask))


def scatter_core(left, right, *small):
    sent, kept = row_grads(lax.axis_index(SHARD) % 2, left, right, *small)
    return kept, swap(sent, SHARD, 1)


def scatter_rest(left, right):
    far, _, side = spots()
    both = lambda bit, pair, dim: wide(pick(bit, pair[0], dim)) + wide(pick(bit, pair[1], dim))
    left = both(far, left, 0) + wide(swap(low(both(1 - far, left, 0)), SHARD, 2))
    right = both(side, right, 1) + wide(swap(low(both(1 - side, right, 1)), CTX, 1))
    return added(CTX, 1, side, left, 0), added(SHARD, 2, far, right, 0)


def spread_tp(chunk):
    return [chunk] + [swap(chunk, TP, step) for step in range(1, lax.axis_size(TP))]


def spread_steps(chunk):
    return [chunk] + [swap(chunk, TP, step) for step in range(1, lax.axis_size(TP))]


def join_tp(pieces, kind):
    part = lax.axis_index(TP)
    rows = pieces[0].shape[0]
    joined = jnp.zeros((len(pieces) * rows,) + pieces[0].shape[1:], kind)
    for step, piece in enumerate(pieces):
        joined = lax.dynamic_update_slice_in_dim(joined, piece.astype(kind), (part ^ step) * rows, 0)
    return joined


def join_wide(pieces):
    part = lax.axis_index(TP)
    columns = pieces[0].shape[1]
    joined = jnp.zeros((pieces[0].shape[0], len(pieces) * columns), pieces[0].dtype)
    for step, piece in enumerate(pieces):
        joined = lax.dynamic_update_slice_in_dim(joined, piece, (part ^ step) * columns, 1)
    return joined


def trade_wide(values, more=None):
    part, count = lax.axis_index(TP), lax.axis_size(TP)
    columns = values.shape[1] // count
    moved = []
    for step in range(count):
        piece = lax.dynamic_slice_in_dim(values, (part ^ step) * columns, columns, 1)
        if more is not None:
            piece = jnp.concatenate((piece, more), axis=1)
        moved.append(swap(piece, TP, step) if step else piece)
    return moved


def total_of(pieces):
    total = wide(pieces[0])
    for piece in pieces[1:]:
        total = total + wide(piece)
    return total


def trade_tp(pieces):
    part = lax.axis_index(TP)
    moved = [pick(part, pieces, 0)]
    for step in range(1, pieces.shape[0]):
        moved.append(swap(pick(part ^ step, pieces, 0), TP, step))
    return moved


def sum_tp(pieces):
    moved = trade_tp(pieces)
    total = wide(moved[0])
    for piece in moved[1:]:
        total = total + wide(piece)
    return total


def after(value, *others):
    return lax.optimization_barrier((value,) + others)[0]


def join_ctx(own, other):
    return ordered(lax.axis_index(CTX), own, other, 0).reshape(-1, own.shape[1])


def scatter_ctx(grads):
    side = lax.axis_index(CTX)
    return added(CTX, 1, side, grads.reshape(2, -1, grads.shape[1]), 0)


def place_maps(routes, pair_order, experts, capacity):
    tok_rows = routes.shape[0]
    flat_route = routes.T.reshape(-1)
    flat_order = pair_order.T.reshape(-1)
    onehot = flat_route[None, :] == jnp.arange(experts, dtype=jnp.int32)[:, None]
    before = low(flat_order[:, None] < flat_order[None, :])
    earlier = mul(low(onehot), before)
    position = jnp.sum(jnp.where(onehot, earlier, 0.0), axis=0)
    slot = jnp.where(position < capacity, position, -1.0)
    split_hot = onehot.reshape(experts, 2, tok_rows)
    places = jnp.sum(jnp.where(split_hot, slot.reshape(1, 2, tok_rows) + 1.0, 0.0), axis=1) - 1.0
    others = jnp.sum(jnp.where(split_hot, wide(flat_route.reshape(1, 2, tok_rows)[:, ::-1]), 0.0), axis=1)
    return places, others


def hot_places(places, capacity):
    slots = jnp.arange(capacity, dtype=jnp.float32)
    return low(places[..., None, :] == slots[:, None])


def all_shards(block):
    beyond = swap(block, SHARD, 2)
    return block, swap(block, SHARD, 1), beyond, swap(beyond, SHARD, 1)


def norm_back(grads, scaled, inv_root, gain):
    slope = grads * gain
    return inv_root * (slope - scaled * jnp.mean(slope * scaled, axis=-1, keepdims=True))


def gelu_gate(gate_pre, up_pre):
    return jax.nn.gelu(gate_pre, approximate=True) * up_pre


def layer(
    tokens, cotangent, segment_ids, routes, pair_order, rel_bucket, attn_gain, w_query, w_key, w_value, w_output,
    bias_table, ffn_gain, w_router, expert_gate, expert_up, expert_down,
):
    shard, side, part = lax.axis_index(SHARD), lax.axis_index(CTX), lax.axis_index(TP)
    shards, tp_count = lax.axis_size(SHARD), lax.axis_size(TP)
    tok_rows, model_width = tokens.shape
    experts = w_router.shape[1]
    capacity = 9 * 2 * tok_rows // (8 * experts)
    local_width = w_query.shape[1]
    chunk_rows = tok_rows // tp_count
    four = quad()

    small_count = 2 + experts
    small_rows = -(-small_count // 16) * 16
    small = jnp.concatenate((attn_gain[None], ffn_gain[None], w_router.T), axis=0)
    small = jnp.pad(small, ((0, small_rows - small_count), (0, 0)))
    rows_in = wide(tokens)
    root_one = lax.rsqrt(jnp.mean(rows_in * rows_in, axis=-1, keepdims=True) + EPSILON)
    joined_block = jnp.concatenate((w_query, w_key, w_value), axis=1)
    if four:
        spot = jnp.stack((shard // 2, shard % 2, side, part))
        half = joined_block.shape[1] // 2
        left = jnp.concatenate((joined_block[:, :half], jnp.pad(small, ((0, 0), (0, half - small.shape[1])))), axis=0)
        first = stage_one(left, joined_block[:, half:])
        joined_parts = stage_three(first, stage_two(*first))
        places, others = place_maps(routes, pair_order, experts, capacity)
        route_maps = after(jnp.stack((places, others), axis=1), *first)
        sent_maps = lax.all_to_all(route_maps, SHARD, split_axis=0, concat_axis=0, tiled=True)
        query_rows, own_pair, joined_w, normed, small_all = project(spot, after(tokens, sent_maps), joined_parts)
    else:
        small_all = gather_rows(small).reshape(-1, small_rows, small.shape[1])
        small_all = jnp.swapaxes(small_all, 0, 1).reshape(small_rows, model_width)
        normed = low(rows_in * root_one * wide(small_all[0]))
        joined_w = gather_rows(joined_block)
        projected = low(mul(normed, joined_w))
        query_rows = low(projected[:, :local_width] * 0.125)
        own_pair = projected[:, local_width:]
        places, others = place_maps(routes, pair_order, experts, capacity)
        route_maps = jnp.stack((places, others), axis=1)
        sent_maps = lax.all_to_all(route_maps, SHARD, split_axis=0, concat_axis=0, tiled=True)
    gain_attn, gain_ffn = wide(small_all[0]), wide(small_all[1])
    router_rows = small_all[2 : 2 + experts]
    far_pair = swap(own_pair, CTX, 1)
    output_pieces = spread_tp(w_output)
    if four:
        output_left = jnp.concatenate(output_pieces[: tp_count // 2], axis=1)
        output_right = jnp.concatenate(output_pieces[tp_count // 2 :], axis=1)
        first = stage_one(output_left, output_right)
        output_w = laid(spot, stage_three(first, stage_two(*first)), model_width, tp_count // 2)
    else:
        output_w = gather_rows(join_wide(output_pieces))

    if four:
        sent_maps = sent_maps[jnp.arange(shards) ^ shard]
    hot = hot_places(sent_maps[:, 0], capacity)
    other_slot = jnp.sum(jnp.where(hot > 0, sent_maps[:, 1][:, None, :], 0.0), axis=2).reshape(-1)

    halves = []
    for block in (expert_down, expert_gate, expert_up):
        halves.append((block[0].T, swap(after(block[0].T, own_pair), CTX, 1)))
    halves = halves[1:] + halves[:1]
    segments = segment_ids[0]
    seg_own = lax.dynamic_slice_in_dim(segments, side * tok_rows, tok_rows)
    seg_far = lax.dynamic_slice_in_dim(segments, (1 - side) * tok_rows, tok_rows)
    buckets = jnp.pad(rel_bucket, (1, 0), constant_values=-1)
    bucket_hot = low(buckets[:, None] == jnp.arange(bias_table.shape[0], dtype=jnp.int32)[None, :])
    near_hot = bucket_hot[tok_rows : 3 * tok_rows][::-1]
    beyond_hot = lax.dynamic_slice_in_dim(bucket_hot, 2 * tok_rows * (1 - side), 2 * tok_rows)[::-1]
    heads = bias_table.shape[1]
    near = ein("qb,bh->hq", near_hot, bias_table).reshape(heads // 2, 2, -1)
    beyond = ein("qb,bh->hq", beyond_hot, bias_table).reshape(heads // 2, 2, -1)
    masks = (seg_own[None, :], seg_own[:, None], seg_far[:, None], near, beyond)
    context, log_totals = attend(query_rows, own_pair, far_pair, *masks)
    context_all = join_wide(trade_tp(context.reshape(tp_count, chunk_rows, local_width)))

    chunk_in = lax.dynamic_slice_in_dim(rows_in, part * chunk_rows, chunk_rows, 0)
    chunk_grad = wide(lax.dynamic_slice_in_dim(cotangent, part * chunk_rows, chunk_rows, 0))
    hidden = chunk_in + ein("th,dh->td", context_all, output_w)
    root_two = lax.rsqrt(jnp.mean(hidden * hidden, axis=-1, keepdims=True) + EPSILON)
    scaled_two = hidden * root_two
    moe_in = low(scaled_two * gain_ffn)

    side_row = side[None]
    if four:
        shard_grads = all_shards(after(cotangent, own_pair))
        grad_rows, out_slope = slopes(side_row, sent_maps[:, 0], *halves[2], shard_grads, capacity)
        chunk_places = sent_maps[:, 0].reshape(shards, tp_count, chunk_rows)[:, jnp.arange(tp_count) ^ part]
        chunk_places = chunk_places[:, ::-1]
        blocks = [all_shards(piece) for piece in spread_steps(moe_in)]
        blocks = blocks[::-1]
        own_hot = (jnp.arange(8, dtype=jnp.int32) == shard).astype(jnp.float32)[None]
        router_pad = jnp.pad(router_rows, ((0, 8 - experts), (0, 0)))
        (expert_rows, gate_low, up_low, weighted), sent, kept = expert(
            jnp.stack((side, shard)), chunk_places, other_slot[:, None], own_hot, router_pad, *halves[:2], out_slope, blocks, BACK_GROUPS
        )
    else:
        gate_w, up_w, down_w = (join_ctx(own.T, other.T) for own, other in halves)
        own_hot = hot_places(places, capacity)
        grad_rows = low(ein("ect,td->ecd", own_hot, cotangent))
        grad_rows = lax.all_to_all(grad_rows, SHARD, split_axis=0, concat_axis=0, tiled=True).reshape(-1, model_width)
        spread = join_tp(spread_tp(moe_in), jnp.bfloat16)
        expert_rows = low(ein("ect,td->ecd", own_hot, spread))
        expert_rows = lax.all_to_all(expert_rows, SHARD, split_axis=0, concat_axis=0, tiled=True).reshape(-1, model_width)
        slot_logits = ein("sd,ed->se", expert_rows, router_rows)
        ids = jnp.arange(experts, dtype=jnp.float32)
        own_logit = jnp.sum(jnp.where(ids[None, :] == wide(shard), slot_logits, 0.0), axis=1)
        other_logit = jnp.sum(jnp.where(ids[None, :] == other_slot[:, None], slot_logits, 0.0), axis=1)
        slot_gate = jax.nn.softmax(jnp.stack((own_logit, other_logit), axis=1), axis=1)[:, :1]
        out_slope = mul(grad_rows, down_w)
        product, pull_gate = jax.vjp(gelu_gate, mul(expert_rows, gate_w), mul(expert_rows, up_w))
        activated = low(product)
        grad_gate_pre, grad_up_pre = pull_gate(wide(low(slot_gate * out_slope)))
        gate_low, up_low = low(grad_gate_pre), low(grad_up_pre)
        gate_slopes = jnp.sum(out_slope * wide(activated), axis=1)
        weighted = low(slot_gate * wide(activated))
        token_slopes = jnp.sum(wide(hot) * gate_slopes.reshape(shards, capacity)[:, :, None], axis=1)

    def combine(kept, received, sizes):
        order = 0
        owns, pieces = [], []
        for own, near, size in zip(kept, received, sizes):
            far = swap(low(wide(own[1]) + wide(near[1])), SHARD, 2)
            own = low(wide(own[0]) + wide(near[0]) + wide(far))
            owns.append(own)
            own = own.reshape(size, -1, model_width)
            for index in range(size):
                step = tp_count - 1 - order
                order += 1
                piece = own[index]
                pieces.append(swap(piece, TP, step) if step else piece)
        return pieces, owns

    def combine_plain(slot_values):
        back = slot_values.reshape(shards, capacity, model_width)
        back = lax.all_to_all(back, SHARD, split_axis=0, concat_axis=0, tiled=True)
        mixed = low(ein("ect,ecd->td", own_hot, back))
        return sum_tp(mixed.reshape(tp_count, chunk_rows, model_width))

    if four:
        received = [swap(block, SHARD, 1) for block in sent]
        back_pieces, back_owns = combine(kept, received, BACK_GROUPS)
        layer_sent, layer_kept = outputs(side_row, chunk_places, after(weighted, *back_owns), *halves[2], LAYER_GROUPS)
        layer_near = [swap(block, SHARD, 1) for block in layer_sent]
        sent_grads, kept_grads = weight_grads(
            side_row, after(expert_rows, *received), grad_rows, gate_low, up_low, weighted
        )
        grad_moe_in = total_of(back_pieces)
        token_slopes = grad_moe_in[chunk_rows].reshape(-1, chunk_rows)[:experts]
        grad_moe_in = grad_moe_in[:chunk_rows]
    else:
        grad_moe_in = combine_plain(low(ein("sf,df->sd", gate_low, gate_w) + ein("sf,df->sd", up_low, up_w)))
        token_slopes = lax.all_to_all(token_slopes, SHARD, split_axis=0, concat_axis=0, tiled=True)
        token_slopes = jnp.swapaxes(token_slopes.reshape(experts, tp_count, chunk_rows), 0, 1)
        token_slopes = sum_tp(token_slopes)

    chunk_routes = lax.dynamic_slice_in_dim(routes, part * chunk_rows, chunk_rows, 0)
    route_hot = chunk_routes[:, :, None] == jnp.arange(experts, dtype=jnp.int32)[None, None, :]
    logits = ein("td,ed->te", moe_in, router_rows)
    gate_values = jax.nn.softmax(jnp.sum(jnp.where(route_hot, logits[:, None, :], 0.0), axis=2), axis=1)
    grad_gates = jnp.sum(jnp.where(route_hot, token_slopes.T[:, None, :], 0.0), axis=2)
    grad_chosen = gate_values * (grad_gates - jnp.sum(gate_values * grad_gates, axis=1, keepdims=True))
    grad_logits = low(jnp.sum(jnp.where(route_hot, grad_chosen[:, :, None], 0.0), axis=1))
    grad_normed_two = grad_moe_in + ein("te,ed->td", grad_logits, router_rows)
    grad_hidden = chunk_grad + norm_back(grad_normed_two, scaled_two, root_two, gain_ffn)
    grad_branch = low(grad_hidden)
    grad_context = low(mul(grad_branch, output_w))
    grad_context = join_tp(trade_wide(grad_context), jnp.bfloat16)
    router_part = ein("te,td->ed", grad_logits, moe_in)
    ffn_gain_part = jnp.sum(grad_normed_two * scaled_two, axis=0)

    if four:
        layer_pieces, _ = combine(layer_kept, layer_near, LAYER_GROUPS)
        layer_part = total_of(lax.optimization_barrier((grad_context, *layer_pieces))[1:])
    else:
        layer_part = combine_plain(low(ein("sf,df->sd", weighted, down_w)))
        expert_grads = [
            scatter_ctx(ein("sd,sf->df", left, right))
            for left, right in ((expert_rows, gate_low), (expert_rows, up_low), (grad_rows, weighted))
        ]
    layer_chunk = low(hidden + layer_part)
    layer_spread = spread_tp(layer_chunk)

    query_grad, pair_own, pair_far, bands = attend_back(query_rows, grad_context, own_pair, far_pair, *masks, log_totals)
    received = swap(pair_far, CTX, 1)
    pair_grad = low(pair_own + wide(received))
    joined_grad = jnp.concatenate((query_grad, pair_grad[0], pair_grad[1]), axis=1)
    grad_normed = ein("th,dh->td", joined_grad, joined_w)
    scaled_one = rows_in * root_one
    attn_gain_part = jnp.sum(grad_normed * scaled_one, axis=0)
    moved = trade_tp(low(grad_normed).reshape(tp_count, chunk_rows, model_width))

    bands = bands.reshape(heads // 2, 2, 2, -1)
    near_band = bands[:, 0].reshape(heads, -1)
    far_band = bands[:, 1].reshape(heads, -1)
    table_part = jnp.dot(wide(near_hot).T, near_band.T, precision=HIGHEST_PRECISION) + jnp.dot(
        wide(beyond_hot).T, far_band.T, precision=HIGHEST_PRECISION
    )
    table_column = jnp.tile(table_part.reshape(-1), model_width // table_part.size)
    small_part = jnp.concatenate((attn_gain_part[None], ffn_gain_part[None], router_part), axis=0)

    if four:
        small_part = jnp.concatenate((small_part, table_column[None]), axis=0)
        small_part = jnp.pad(small_part, ((0, 128 - small_part.shape[0]), (0, 0))).T
        output_four = scatter_core(after(grad_branch, pair_far), context_all)
        joined_four = scatter_core(normed, joined_grad, small_part)
        expert_grads = [(kept_part, swap(sent_part, CTX, 1)) for kept_part, sent_part in zip(kept_grads, sent_grads)]
        held = lax.optimization_barrier((layer_chunk, *output_four, *joined_four, *moved))
        output_four, joined_four, moved = held[1:3], held[3:5], held[5:]
    chunk_normed = total_of(moved)
    chunk_scaled = lax.dynamic_slice_in_dim(scaled_one, part * chunk_rows, chunk_rows, 0)
    chunk_root = lax.dynamic_slice_in_dim(root_one, part * chunk_rows, chunk_rows, 0)
    chunk_tokens = low(grad_hidden + norm_back(chunk_normed, chunk_scaled, chunk_root, gain_attn))
    token_pieces = spread_tp(chunk_tokens)
    if four:
        grad_output_w, rest = scatter_rest(output_four, (after(joined_four[0], chunk_tokens), joined_four[1]))
        grad_joined, small_rest = rest[:, : 3 * local_width], rest[:, 3 * local_width :]
        summed = total_of(trade_wide(low(grad_output_w), low(small_rest)))
        table_sum = small_rest[:, small_count]
        expert_grads = [(after(kept_part, chunk_tokens) + wide(near)).T for kept_part, near in expert_grads]
        held = lax.optimization_barrier((grad_joined, summed, *expert_grads, layer_spread[0]))
        grad_joined, summed, expert_grads = held[0], held[1], held[2:5]
        layer_out = join_rows(part, [held[5]] + layer_spread[1:], jnp.bfloat16)
        grad_output_w, small_sum = summed[:, :local_width], summed[:, local_width : local_width + small_count].T
        tokens_grad = join_rows(part, token_pieces, jnp.float32)
    else:
        scatter = lambda values: lax.psum_scatter(values, (SHARD, CTX), scatter_dimension=0, tiled=True)
        grad_output_w = total_of(trade_wide(low(scatter(ein("td,th->dh", grad_branch, context_all)))))
        grad_joined = scatter(ein("td,th->dh", normed, joined_grad))
        small_sum = lax.psum(scatter(small_part.T).T, TP)
        table_sum = lax.psum(table_part, (SHARD, CTX))
        layer_out = join_tp(layer_spread, jnp.bfloat16)
        tokens_grad = join_tp(token_pieces, jnp.float32)
    return (
        layer_out,
        tokens_grad,
        small_sum[0],
        grad_joined[:, :local_width],
        grad_joined[:, local_width : 2 * local_width],
        grad_joined[:, 2 * local_width :],
        grad_output_w,
        table_sum.reshape(bias_table.shape),
        small_sum[1],
        small_sum[2:].T,
        expert_grads[0][None],
        expert_grads[1][None],
        expert_grads[2][None],
    )


def solution(mesh):
    return jax.shard_map(
        layer,
        mesh=mesh,
        in_specs=(
            P((SHARD, CTX), None),
            P((SHARD, CTX), None),
            P(SHARD, None),
            P((SHARD, CTX), None),
            P((SHARD, CTX), None),
            P(),
            P((SHARD, CTX)),
            P((SHARD, CTX), TP),
            P((SHARD, CTX), TP),
            P((SHARD, CTX), TP),
            P((SHARD, CTX), TP),
            P(None, TP),
            P((SHARD, CTX)),
            P((SHARD, CTX), None),
            P(SHARD, CTX, TP),
            P(SHARD, CTX, TP),
            P(SHARD, CTX, TP),
        ),
        out_specs=(
            P((SHARD, CTX), None),
            P((SHARD, CTX), None),
            P((SHARD, CTX)),
            P((SHARD, CTX), TP),
            P((SHARD, CTX), TP),
            P((SHARD, CTX), TP),
            P((SHARD, CTX), TP),
            P(None, TP),
            P((SHARD, CTX)),
            P((SHARD, CTX), None),
            P(SHARD, CTX, TP),
            P(SHARD, CTX, TP),
            P(SHARD, CTX, TP),
        ),
        check_vma=False,
    )
```
